128 devices in a mesh: sec: 2 (over core), dev: 64 (over z, x, y).
Axes of the slice: x: 4, y: 4, z: 4, core: 2. Of those that a mesh axis runs over, the one named last changes fastest.
Arguments:
- queries: bfloat16 [256, 4, 6144], P('dev'), may hold values from -160 to 160
- cache_keys: bfloat16 [256, 128, 1024], P('dev'), may hold values from -8 to 8
- cache_values: bfloat16 [256, 128, 1024], P('dev'), may hold values from -6 to 6
- lengths: int32 [256], P('dev'), may hold values from 1 to 128, 16384 in all
- new_keys: bfloat16 [256, 4, 1024], P('dev'), may hold values from -6 to 6
- new_values: bfloat16 [256, 4, 1024], P('dev'), may hold values from -6 to 6
- residual: bfloat16 [256, 4, 6144], P('dev'), may hold values from -6 to 6
- norm_gain: float32 [6144], replicated, may hold values from 0.25 to 1.75
- expert_ids: int32 [1024, 2], P('dev'), may hold values from 0 to 3, all different within a row; in each aligned block of 16 rows (0 to 15, 16 to 31, ...) at most 9 rows name the same one
- gate_logits: float32 [1024, 2], P('dev'), may hold values from -8 to 8
- w_gate: bfloat16 [6144, 32768], P(None, 'dev'), may hold values from -0.078125 to 0.078125
- w_up: bfloat16 [6144, 32768], P(None, 'dev'), may hold values from -0.078125 to 0.078125
- w_down: bfloat16 [32768, 6144], P('dev'), may hold values from -0.0625 to 0.0625
Outputs:
- layer_out: bfloat16 [256, 4, 6144], P('dev', None, 'sec')
The draws below stay inside these ranges and needn't reach their ends.
Inputs may be any that keep to these rules, and one draw needn't show every extreme that they name: `expert_ids`: in the 16 tokens of one attention device no expert is named more than 9 times; some expert is named exactly 9 times in some of these blocks.
All inputs are finite; a program needn't handle non-finite values. No bound on the sum of `lengths` on one device may be relied on, other than what follows from the above.
Results may differ from the reference program's by a relative error of at most 0.0065.
Values may be sent and summed in bfloat16 or wider, within the bound.
A program may use at most 192 MiB of HBM per device.

```python
import math
import jax
import jax.numpy as jnp
import numpy as np
from jax import lax

D = 6144
HEADS = 48
KVH = 8
HD = 128
EXP = 4
FF = 8192
STEPS = 4
LMAX = 128
REQUESTS = 256
TOKD = 16
TOKENS = 1024
CAP = 9
N_DEV = 64


def cache_normal(key):
    return jax.random.normal(jax.random.fold_in(key, 11), (REQUESTS, LMAX, KVH * HD), jnp.float32)


def draw_cache_keys(key, part):
    base = cache_normal(key)
    return base.astype(jnp.bfloat16)


def draw_queries(key, part):
    fresh = jax.random.normal(jax.random.fold_in(key, 23), (REQUESTS, STEPS, HEADS * HD), jnp.float32)
    return fresh.astype(jnp.bfloat16)


def shard_levels(rng, shape, cuts, least, top_value):
    loudness = 1.0
    for dim, blocks in cuts:
        steps = jax.random.uniform(jax.random.fold_in(jax.random.fold_in(rng, 6), dim), (blocks,), jnp.float32, least / len(cuts), top_value / len(cuts))
        loudness = loudness * jnp.repeat(jnp.exp(steps), shape[dim] // blocks).reshape((-1,) + (1,) * (len(shape) - 1 - dim))
    return loudness


def profile(amount, total, most, slope):
    portions = [(1 << 20) // math.isqrt(rank ** slope) + 1 for rank in range(2, amount + 1)]
    surplus, holding = total - most - (amount - 1), [1] * (amount - 1)
    while surplus > 0:
        free = [i for i in range(amount - 1) if holding[i] < most]
        mass, left = sum([portions[i] for i in free]), surplus
        for i in free:
            addition = min(most - holding[i], max(1, left * portions[i] // mass), surplus)
            holding[i] = holding[i] + addition
            surplus = surplus - addition
    return np.array([most] + holding)


def uneven_parts(stream_key, amount, total, limit, lean):
    if amount == 2:
        one = jax.random.randint(stream_key, (), max(1, total - limit), min(limit, total - 1) + 1)
        return jnp.stack([one, total - one])
    tallies = jnp.asarray(profile(amount, total, limit, lean), jnp.int32)
    couples = (amount - 1) // 2
    source_of, receiver = tallies[1:1 + 2 * couples:2], tallies[2:2 + 2 * couples:2]
    margin = jnp.minimum(source_of - 1, limit - receiver)
    shifted = jax.random.randint(jax.random.fold_in(stream_key, 1), (couples,), 0, 1 << 20) % (margin + 1)
    tallies = tallies.at[1:1 + 2 * couples:2].set(source_of - shifted).at[2:2 + 2 * couples:2].set(receiver + shifted)
    return tallies[jax.random.permutation(jax.random.fold_in(stream_key, 2), amount)]


def deal_out(key, own, number, rows, count, top, reach, slope):
    ranking = jax.random.permutation(key, count)
    heavy_load, ordinary = shares(count, rows * top, reach, slope, True), shares(count, rows * top, reach, slope, False)
    places = jnp.arange(count)

    def named(tallies, offset_by):
        used = int((tallies > 0).sum())
        fixed = max(1, used // 4)
        passed = fixed + (places - fixed + offset_by * (used - fixed)) % max(1, count - fixed)
        return jnp.zeros((count,), jnp.int32).at[ranking[jnp.where(places < fixed, places, passed)]].set(jnp.asarray(tallies, jnp.int32))

    tallies = jnp.where(number % 4 == 0, named(heavy_load, number // 4), named(ordinary, number - number // 4 - 1))
    mixed = jax.random.permutation(jax.random.fold_in(own, 3), count)
    donor, taker = mixed[0:count // 2 * 2:2], mixed[1:count // 2 * 2:2]
    margin = jnp.minimum(tallies[donor] - 1, reach - tallies[taker]) // 2
    margin = jnp.where((donor == ranking[0]) | (taker == ranking[0]) | (tallies[taker] == 0), 0, jnp.maximum(margin, 0))
    passed = jax.random.randint(jax.random.fold_in(own, 4), (count // 2,), 0, 1 << 20) % (margin + 1)
    tallies = tallies.at[donor].add(-passed).at[taker].add(passed)
    items = jnp.searchsorted(jnp.cumsum(tallies), jnp.arange(rows * top), side="right").astype(jnp.int32)
    listing = items.reshape(top, rows).T
    listing = listing[jax.random.permutation(jax.random.fold_in(own, 1), rows)]
    offset_by = jax.random.randint(jax.random.fold_in(own, 2), (rows, 1), 0, top)
    return jnp.take_along_axis(listing, (jnp.arange(top)[None, :] + offset_by) % top, axis=1)


def shares(number_of, total, most, slope, full):
    loads = [(1 << 20) // math.isqrt(rank ** slope) + 1 for rank in range(1, number_of + 1)]
    largest = most if full else min(most, max(-(-total // number_of), total * loads[0] // sum(loads)))
    least = 1 if total - largest >= number_of - 1 else 0
    counts, spare = [largest] + [least] * (number_of - 1), total - largest - least * (number_of - 1)
    while spare > 0:
        movable = [i for i in range(1, number_of) if counts[i] < largest] or [i for i in range(1, number_of) if counts[i] < most]
        whole, budget = sum([loads[i] for i in movable]), spare
        for i in movable:
            extra = min(most - counts[i], max(1, budget * loads[i] // whole), spare)
            counts[i] = counts[i] + extra
            spare = spare - extra
    return np.array(counts)


def gaussian(key, extent, spread, reach, shards=(), kind=jnp.bfloat16):
    values = jax.random.normal(key, extent, jnp.float32) * spread
    if len(shards) > 0:
        values = shard_levels(key, extent, shards, -0.22, 0.18) * values
    return jnp.clip(values, min=-reach, max=reach).astype(kind)


def setup_inputs(seed: int = 0) -> dict:
    key_of = jax.random.split(jax.random.key(seed), 14)
    queries = draw_queries(jax.random.fold_in(key_of[13], 71), 0)
    cache_keys = draw_cache_keys(jax.random.fold_in(key_of[13], 71), 0)
    cache_values = gaussian(key_of[2], (REQUESTS, LMAX, KVH * HD), 1.0, 6.0, ((0, 64),))
    lengths = uneven_parts(key_of[3], REQUESTS, REQUESTS * LMAX // 2, LMAX, 1).astype(jnp.int32)
    new_keys = gaussian(key_of[4], (REQUESTS, STEPS, KVH * HD), 1.0, 6.0, ((0, 64),))
    new_values = gaussian(key_of[5], (REQUESTS, STEPS, KVH * HD), 1.0, 6.0, ((0, 64),))
    residual = gaussian(key_of[6], (REQUESTS, STEPS, D), 1.0, 6.0, ((0, 64),))
    norm_gain = jnp.clip(1.0 + 0.15 * jax.random.normal(key_of[7], (D,), jnp.float32), 0.25, 1.75)
    expert_ids_keys = jax.random.split(jax.random.fold_in(key_of[8], 1), TOKENS // TOKD)
    expert_ids_turns = jax.random.permutation(jax.random.fold_in(key_of[8], 3), TOKENS // TOKD)
    expert_ids = jax.vmap(lambda own, number: deal_out(jax.random.fold_in(key_of[8], 2), own, number, TOKD, EXP, 2, CAP, 2))(expert_ids_keys, expert_ids_turns).reshape((TOKENS, 2))
    gate_logits = gaussian(key_of[9], (TOKENS, 2), 1.5, 8.0, ((0, 64),), jnp.float32)
    w_gate = gaussian(key_of[10], (D, EXP * FF), D ** -0.5, 0.078125, ((1, 64),))
    w_up = gaussian(key_of[11], (D, EXP * FF), D ** -0.5, 0.078125, ((1, 64),))
    w_down = gaussian(key_of[12], (EXP * FF, D), FF ** -0.5, 0.0625, ((0, 64),))
    return {"queries": queries, "cache_keys": cache_keys, "cache_values": cache_values, "lengths": lengths, "new_keys": new_keys, "new_values": new_values, "residual": residual, "norm_gain": norm_gain, "expert_ids": expert_ids, "gate_logits": gate_logits, "w_gate": w_gate, "w_up": w_up, "w_down": w_down}


def expert_output(normed_rows, gate_stack, up_stack, down_stack):

    def one_slice(total, pieces):
        gate_piece, up_piece, down_piece = pieces
        gate = jnp.dot(normed_rows, gate_piece, preferred_element_type=jnp.float32)
        upward = jnp.dot(normed_rows, up_piece, preferred_element_type=jnp.float32)
        hidden = (jax.nn.silu(gate) * upward).astype(jnp.bfloat16)
        part = jnp.dot(hidden, down_piece, preferred_element_type=jnp.float32).astype(jnp.bfloat16)
        return (total + part.astype(jnp.float32), None)
    start = jnp.zeros((normed_rows.shape[0], D), jnp.float32)
    total, _ = lax.scan(one_slice, start, (gate_stack, up_stack, down_stack))
    return total

def reference(queries, cache_keys, cache_values, lengths, new_keys, new_values, residual, norm_gain, expert_ids, gate_logits, w_gate, w_up, w_down):
    per_group = HEADS // KVH
    key_all = jnp.concatenate([cache_keys, new_keys], axis=1).astype(jnp.float32).reshape(REQUESTS, LMAX + STEPS, KVH, HD)
    value_all = jnp.concatenate([cache_values, new_values], axis=1).astype(jnp.float32).reshape(REQUESTS, LMAX + STEPS, KVH, HD)
    query_heads = queries.astype(jnp.float32).reshape(REQUESTS, STEPS, KVH, per_group, HD)
    scores = jnp.einsum('rsgqd,rlgd->rsgql', query_heads, key_all) * HD ** (-0.5)
    position = jnp.arange(LMAX + STEPS, dtype=jnp.int32)
    stepnum = jnp.arange(STEPS, dtype=jnp.int32)
    in_cache = position[None, None, :] < lengths[:, None, None]
    in_window = (position[None, :] >= LMAX) & (position[None, :] - LMAX <= stepnum[:, None])
    valid = in_cache | in_window[None, :, :]
    scores = jnp.where(valid[:, :, None, None, :], scores, jnp.float32(-1e+30))
    peak = lax.optimization_barrier(jnp.max(scores, axis=-1, keepdims=True))
    expo = jnp.exp(scores - peak)
    probs = (expo / lax.optimization_barrier(jnp.sum(expo, axis=-1, keepdims=True))).astype(jnp.bfloat16)
    attended = jnp.einsum('rsgql,rlgd->rsgqd', probs.astype(jnp.float32), value_all).reshape(REQUESTS, STEPS, D)
    hstate = (residual.astype(jnp.float32) + attended).astype(jnp.bfloat16)
    hfloat = hstate.astype(jnp.float32)
    meansq = lax.optimization_barrier(jnp.mean(hfloat * hfloat, axis=-1, keepdims=True))
    moe_in = (hfloat * lax.rsqrt(meansq + 1e-05) * norm_gain).astype(jnp.bfloat16)
    flat_in = moe_in.reshape(TOKENS, D)
    group = N_DEV // EXP
    slice_width = FF // group
    weights = jax.nn.softmax(gate_logits, axis=-1)
    mixed = jnp.zeros((TOKENS, D), jnp.float32)
    for expert in range(EXP):
        gate_stack = w_gate[:, expert * FF:(expert + 1) * FF].reshape(D, group, slice_width).transpose(1, 0, 2)
        up_stack = w_up[:, expert * FF:(expert + 1) * FF].reshape(D, group, slice_width).transpose(1, 0, 2)
        down_stack = w_down[expert * FF:(expert + 1) * FF, :].reshape(group, slice_width, D)
        result = expert_output(flat_in, gate_stack, up_stack, down_stack)
        factor = lax.optimization_barrier(jnp.sum(weights * (expert_ids == expert).astype(jnp.float32), axis=1))
        mixed = mixed + factor[:, None] * result
    layer_out = (hstate.reshape(TOKENS, D).astype(jnp.float32) + mixed).astype(jnp.bfloat16)
    return layer_out.reshape(REQUESTS, STEPS, D)
```

```python
import functools

import jax
import jax.numpy as jnp
from jax import lax
from jax.experimental import pallas as pl
from jax.experimental.pallas import tpu as pltpu
from jax.sharding import PartitionSpec as P

HEADS = 48
KVH = 8
HD = 128
EXP = 4
LMAX = 128
CAP = 9
SIDE = 4
EPS = 1e-05

F32 = jnp.float32
BF16 = jnp.bfloat16
HALF = 3072
FF = 512
FA = 1408
FB = HALF - FA
NSEM = 200
TILE = 256
GROUPS = (
    ((0, 0), (1, 0), (-1, 0), (0, 1), (0, -1)),
    ((1, 1), (1, -1), (-1, 1), (-1, -1), (2, 0), (0, 2)),
    ((2, 1), (2, -1), (1, 2), (-1, 2), (2, 2)),
)


def lanes(j, n=128):
    return slice(j * n, (j + 1) * n)


def kernel(
    lens, q_hbm, k_hbm, v_hbm, nk_hbm, nv_hbm, res_hbm, gain, ids, logits, wg_hbm, wu_hbm, wd_hbm,
    out,
    qb, kb, vb, nkb, nvb, resb, hb, xn, ssb, ssr,
    zs, zr, zos, zor, X, XOs, XO, W, Wd, GU, GUs, GUr, H, Pb, PO, PS,
    ad, af, ad2, af2, bd, bf, bd2, bf2, od, of, od2, of2, rzs, rzr, rzos, rzor,
    lsem, ssem, rsem,
):
    c = lax.axis_index("sec")
    d = lax.axis_index("dev")
    z = d // 16
    x = (d // 4) % 4
    y = d % 4
    here = x * 4 + y

    def near(v, by):
        return lax.rem(v + (by % 4), 4)

    def chip(dz=0, dx=0, dy=0):
        return near(z, dz) * 16 + near(x, dx) * 4 + near(y, dy)

    steps = {"x": lambda by: (c, chip(dx=by)), "y": lambda by: (c, chip(dy=by))}
    zpeers = [(c, chip(dz=k)) for k in (1, 2, 3)]
    sibling = (1 - c, d)
    partners = zpeers + [sibling] + [steps[a](by) for a in ("x", "y") for by in (1, -1)]

    barrier = pltpu.get_barrier_semaphore()
    for p in partners:
        pl.semaphore_signal(barrier, inc=1, device_id=p, device_id_type=pl.DeviceIdType.MESH)

    feats = pl.ds(pl.multiple_of(c * HALF, HALF), HALF)
    kvs = pl.ds(pl.multiple_of(c * 512, 512), 512)
    local = []
    for i, (src, dst) in enumerate((
        (q_hbm.at[:, :, feats], qb),
        (k_hbm.at[:, :, kvs], kb),
        (nk_hbm.at[:, :, kvs], nkb),
        (v_hbm.at[:, :, kvs], vb),
        (nv_hbm.at[:, :, kvs], nvb),
        (res_hbm.at[:, :, feats], resb),
        (wg_hbm.at[feats, :], W.at[:, pl.ds(0, FF)]),
        (wu_hbm.at[feats, :], W.at[:, pl.ds(FF, FF)]),
        (wd_hbm.at[:, feats], Wd),
    )):
        copy = pltpu.make_async_copy(src, dst, lsem.at[i])
        copy.start()
        local.append(copy)

    counter = [0]
    sent = []

    def new_id():
        counter[0] += 1
        return counter[0] - 1

    def send(src, dst, sem, dev):
        copy = pltpu.make_async_remote_copy(
            src_ref=src, dst_ref=dst, send_sem=ssem.at[sem], recv_sem=rsem.at[sem],
            device_id=dev, device_id_type=pl.DeviceIdType.MESH,
        )
        copy.start()
        sent.append(copy)

    def take(dst, sem, dev):
        pltpu.make_async_remote_copy(
            src_ref=dst, dst_ref=dst, send_sem=ssem.at[sem], recv_sem=rsem.at[sem],
            device_id=dev, device_id_type=pl.DeviceIdType.MESH,
        ).wait_recv()

    for copy in local[:6]:
        copy.wait()
    row = lax.broadcasted_iota(jnp.int32, (96, 128), 0)
    col = lax.broadcasted_iota(jnp.int32, (96, 128), 1)
    lenv = jnp.concatenate([jnp.full((24, 128), lens[r], jnp.int32) for r in range(4)], axis=0)
    in_cache = col < lenv
    row16 = lax.broadcasted_iota(jnp.int32, (96, 16), 0)
    col16 = lax.broadcasted_iota(jnp.int32, (96, 16), 1)
    in_window = (row16 // 24 == col16 // 4) & (col16 % 4 <= row16 % 4)
    scale = HD ** (-0.5)
    ss = jnp.zeros((16, 128), F32)
    contract = (((1,), (1,)), ((), ()))
    for g in range(4):
        qs = [
            jnp.concatenate([qb[r, :, lanes(g * 6 + h)].astype(F32) for h in range(6)], axis=0)
            for r in range(4)
        ]
        sc = jnp.concatenate([
            lax.dot_general(qs[r].astype(BF16), kb[r, :, lanes(g)], contract, preferred_element_type=F32)
            for r in range(4)
        ], axis=0) * scale
        nk = jnp.concatenate([nkb[r, :, lanes(g)].astype(F32) for r in range(4)], axis=0).astype(BF16)
        nv = jnp.concatenate([nvb[r, :, lanes(g)].astype(F32) for r in range(4)], axis=0).astype(BF16)
        qa = jnp.concatenate(qs, axis=0).astype(BF16)
        sn = lax.dot_general(qa, nk, contract, preferred_element_type=F32) * scale
        sc = jnp.where(in_cache, sc, -1e30)
        sn = jnp.where(in_window, sn, -1e30)
        peak = jnp.maximum(jnp.max(sc, axis=1, keepdims=True), jnp.max(sn, axis=1, keepdims=True))
        ec = jnp.exp(sc - peak)
        en = jnp.exp(sn - peak)
        total = jnp.sum(ec, axis=1, keepdims=True) + jnp.sum(en, axis=1, keepdims=True)
        inv = 1.0 / total
        pc = ec * inv
        pn = (en * inv).astype(BF16)
        att = jnp.concatenate([
            jnp.dot(pc[24 * r:24 * r + 24].astype(BF16), vb[r, :, lanes(g)], preferred_element_type=F32)
            for r in range(4)
        ], axis=0) + jnp.dot(pn, nv, preferred_element_type=F32)
        for h in range(6):
            j = g * 6 + h
            part = jnp.concatenate([att[r * 24 + h * 4:r * 24 + h * 4 + 4] for r in range(4)], axis=0)
            res = jnp.concatenate([resb[r, :, lanes(j)].astype(F32) for r in range(4)], axis=0)
            hst = (res + part).astype(BF16)
            hb[:, lanes(j)] = hst
            hf = hst.astype(F32)
            ss = ss + hf * hf
    ssb[...] = jnp.broadcast_to(jnp.sum(ss, axis=1, keepdims=True), (16, 128))
    pl.semaphore_wait(barrier, len(partners))
    sid = new_id()
    send(ssb, ssr, sid, sibling)

    idv = ids[...]
    id0, id1 = idv[:, 0:1], idv[:, 1:2]
    slot = lax.broadcasted_iota(jnp.int32, (16, 128), 1)
    who = jnp.where(slot < 32, slot // 8, slot - 32)
    rank = jnp.where(slot < 32, slot % 8, 8)
    hit0 = id0 == who
    hit1 = id1 == who
    hit = jnp.where(hit0 | hit1, 1.0, 0.0)
    before = jnp.where(
        lax.broadcasted_iota(jnp.int32, (16, 16), 1) < lax.broadcasted_iota(jnp.int32, (16, 16), 0), 1.0, 0.0
    )
    ahead = jnp.dot(before.astype(BF16), hit.astype(BF16), preferred_element_type=F32)
    chosen = ahead == rank.astype(F32)
    pick0 = jnp.where(hit0 & chosen, 1.0, 0.0)
    pick1 = jnp.where(hit1 & chosen, 1.0, 0.0)
    packing = jnp.transpose(pick0 + pick1)[0:48].astype(BF16)
    lg = logits[...]
    l0, l1 = lg[:, 0:1], lg[:, 1:2]
    top = jnp.maximum(l0, l1)
    e0, e1 = jnp.exp(l0 - top), jnp.exp(l1 - top)
    w0 = e0 / (e0 + e1)
    w1 = e1 / (e0 + e1)

    take(ssr, sid, sibling)
    inv = lax.rsqrt((ssb[...] + ssr[...]) / (2 * HALF) + EPS)
    gains = gain[pl.ds(pl.multiple_of(c * 24, 8), 24), :]
    for j in range(24):
        xn[:, lanes(j)] = (hb[:, lanes(j)].astype(F32) * inv * gains[j:j + 1]).astype(BF16)
    for n in range(4):
        at = lanes(n, 768)
        packed = jnp.dot(packing, xn[:, at], preferred_element_type=F32)
        for e in range(4):
            zs[e, :, at] = packed[8 * e:8 * e + 8].astype(BF16)
            zos[e, :, at] = packed[32 + e:33 + e]

    zid = [(new_id(), new_id()) for _ in range(3)]
    for k in (1, 3, 2):
        e = near(z, k)
        send(zs.at[e], zr.at[z], zid[k - 1][0], (c, chip(dz=k)))
        send(zos.at[e], zor.at[z], zid[k - 1][1], (c, chip(dz=k)))
    zr[z] = zs[z]
    zor[z] = zos[z]
    for k in (1, 3, 2):
        frm = near(z, -k)
        take(zr.at[frm], zid[k - 1][0], (c, chip(dz=k)))
        take(zor.at[frm], zid[k - 1][1], (c, chip(dz=k)))
    for n in range(4):
        at = lanes(n, 768)
        X[here, :, at] = jnp.concatenate([zr[s, :, at].astype(F32) for s in range(4)], axis=0).astype(BF16)
    for s in range(4):
        XOs[y, s:s + 1, :] = zor[s]

    def blk(dx, dy):
        return near(x, dx) * 4 + near(y, dy)

    class Gather:
        def __init__(self, axis, view, size, cut):
            self.view, self.size, self.cut = view, size, cut
            self.dev = {by: steps[axis](by) for by in (1, -1)}
            self.op, self.om, self.fp, self.fm = new_id(), new_id(), new_id(), new_id()

        def start(self):
            v = self.view(0, 0, self.size)
            send(v, v, self.op, self.dev[1])
            send(v, v, self.om, self.dev[-1])

        def near(self):
            take(self.view(-1, 0, self.size), self.op, self.dev[1])
            v = self.view(-1, 0, self.cut)
            send(v, v, self.fp, self.dev[1])
            take(self.view(1, 0, self.size), self.om, self.dev[-1])
            v = self.view(1, self.cut, self.size - self.cut)
            send(v, v, self.fm, self.dev[-1])

        def far(self):
            take(self.view(2, 0, self.cut), self.fp, self.dev[1])
            take(self.view(2, self.cut, self.size - self.cut), self.fm, self.dev[-1])

    order = (0, 1, -1, 2)
    cut_a = {0: 640, 1: 768, -1: 640, 2: 768}
    cut_b = {0: 768, 1: 896, -1: 768, 2: 896}
    a1 = Gather("y", lambda r, lo, n: X.at[blk(0, r), :, pl.ds(lo, n)], FA, 640)
    b1 = Gather("x", lambda r, lo, n: X.at[blk(r, 0), :, pl.ds(FA + lo, n)], FB, 896)
    o1 = Gather("y", lambda r, lo, n: XOs.at[near(y, r), :, pl.ds(lo, n)], HALF, 1536)
    a2 = {
        k: Gather("x", lambda r, lo, n, k=k: X.at[blk(r, k), :, pl.ds(lo, n)], FA, cut_a[k]) for k in order
    }
    b2 = {
        k: Gather("y", lambda r, lo, n, k=k: X.at[blk(k, r), :, pl.ds(FA + lo, n)], FB, cut_b[k]) for k in order
    }
    o2 = Gather("x", lambda r, lo, n: XO.at[near(x, r), :, pl.ds(lo, n)], HALF, 1536)

    a1.start()
    b1.start()
    o1.start()
    a2[0].start()
    b2[0].start()

    a1.near()
    b1.near()
    for k in (1, -1):
        a2[k].start()
        b2[k].start()
    o1.near()
    a2[0].near()
    b2[0].near()

    place = []
    at = 0
    for n, group in enumerate(GROUPS):
        size = 32 * len(group) + (64 if n == 2 else 0)
        place.append((at, size))
        at += size
    gid = [new_id() for _ in GROUPS]

    def rows_in(n):
        parts = [X[blk(*b)] for b in GROUPS[n]]
        if n == 2:
            parts += [XO[k] for k in range(4)]
        return jnp.concatenate(parts, axis=0)

    def up(n):
        lo, size = place[n]

        @pl.loop(0, 2 * FF // TILE)
        def _(t):
            cols = pl.ds(pl.multiple_of(t * TILE, TILE), TILE)
            acc = jnp.dot(rows_in(n), W[:, cols], preferred_element_type=F32)
            GU[lo:lo + size, cols] = acc
            GUs[lo:lo + size, cols] = acc.astype(BF16)

        v = pl.ds(lo, size)
        send(GUs.at[v], GUr.at[v], gid[n], sibling)

    def down(n):
        lo, size = place[n]
        take(GUr.at[pl.ds(lo, size)], gid[n], sibling)

        @pl.loop(0, size // 32)
        def _(t):
            r = pl.ds(pl.multiple_of(lo + t * 32, 32), 32)
            gate = GU[r, 0:FF] + GUr[r, 0:FF].astype(F32)
            upward = GU[r, FF:2 * FF] + GUr[r, FF:2 * FF].astype(F32)
            H[r, :] = (jax.nn.silu(gate) * upward).astype(BF16)

        @pl.loop(0, HALF // TILE)
        def _(t):
            cols = pl.ds(pl.multiple_of(t * TILE, TILE), TILE)
            acc = jnp.dot(H[lo:lo + size, :], Wd[:, cols], preferred_element_type=F32).astype(BF16)
            for i, b in enumerate(GROUPS[n]):
                Pb[blk(*b), :, cols] = acc[32 * i:32 * i + 32]
            if n == 2:
                base = 32 * len(GROUPS[n])
                for k in range(4):
                    PO[k, :, cols] = acc[base + 16 * k:base + 16 * k + 16]

    for copy in local[6:]:
        copy.wait()
    up(0)
    a1.far()
    a2[2].start()
    b1.far()
    b2[2].start()
    o1.far()
    XO[x] = jnp.concatenate([XOs[k] for k in range(4)], axis=0).astype(BF16)
    o2.start()
    for k in (1, -1):
        a2[k].near()
        b2[k].near()
    o2.near()
    a2[0].far()
    b2[0].far()
    up(1)
    a2[2].near()
    b2[2].near()
    down(0)
    for k in (1, -1):
        a2[k].far()
        b2[k].far()
    o2.far()
    a2[2].far()
    b2[2].far()
    up(2)
    down(1)
    down(2)

    def add_into(dst, srcs):
        n = dst.shape[-1]
        for j in range(n // 128):
            s = pl.ds(j * 128, 128)
            acc = dst[:, s].astype(F32)
            for src in srcs:
                acc = acc + src[:, s].astype(F32)
            dst[:, s] = acc.astype(dst.dtype)

    class Scatter:
        def __init__(self, axis, view, size, cut, dbuf, fbuf):
            self.view, self.size, self.cut = view, size, cut
            self.dev = {by: steps[axis](by) for by in (1, -1)}
            self.dp, self.dm, self.sp, self.sm = new_id(), new_id(), new_id(), new_id()
            self.d = (dbuf(0).at[:, pl.ds(0, cut)], dbuf(1).at[:, pl.ds(0, size - cut)])
            self.f = (fbuf(0), fbuf(1))

        def start(self):
            send(self.view(2, 0, self.cut), self.d[0], self.dp, self.dev[1])
            send(self.view(2, self.cut, self.size - self.cut), self.d[1], self.dm, self.dev[-1])

        def mid(self):
            take(self.d[0], self.dp, self.dev[1])
            add_into(self.view(1, 0, self.cut), [self.d[0]])
            send(self.view(1, 0, self.size), self.f[0], self.sp, self.dev[1])
            take(self.d[1], self.dm, self.dev[-1])
            add_into(self.view(-1, self.cut, self.size - self.cut), [self.d[1]])
            send(self.view(-1, 0, self.size), self.f[1], self.sm, self.dev[-1])

        def fin(self):
            take(self.f[0], self.sp, self.dev[1])
            take(self.f[1], self.sm, self.dev[-1])
            add_into(self.view(0, 0, self.size), self.f)

    ra1, rb1 = {}, {}
    for i, k in enumerate(order):
        ra1[k] = Scatter(
            "x", lambda r, lo, n, k=k: Pb.at[blk(r, k), :, pl.ds(lo, n)], FA, cut_a[k],
            lambda s, i=i: ad.at[i, s], lambda s, i=i: af.at[i, s],
        )
        rb1[k] = Scatter(
            "y", lambda r, lo, n, k=k: Pb.at[blk(k, r), :, pl.ds(FA + lo, n)], FB, cut_b[k],
            lambda s, i=i: bd.at[i, s], lambda s, i=i: bf.at[i, s],
        )
    ra2 = Scatter(
        "y", lambda r, lo, n: Pb.at[blk(0, r), :, pl.ds(lo, n)], FA, 640, lambda s: ad2.at[s], lambda s: af2.at[s]
    )
    rb2 = Scatter(
        "x", lambda r, lo, n: Pb.at[blk(r, 0), :, pl.ds(FA + lo, n)], FB, 896,
        lambda s: bd2.at[s], lambda s: bf2.at[s],
    )
    ro1 = Scatter(
        "x", lambda r, lo, n: PO.at[near(x, r), :, pl.ds(lo, n)], HALF, 1536, lambda s: od.at[s], lambda s: of.at[s]
    )
    ro2 = Scatter(
        "y", lambda r, lo, n: PS.at[near(y, r), :, pl.ds(lo, n)], HALF, 1536, lambda s: od2.at[s], lambda s: of2.at[s]
    )
    back = (2, 1, -1, 0)
    for k in back:
        ra1[k].start()
        rb1[k].start()
    ro1.start()
    for k in back:
        ra1[k].mid()
        rb1[k].mid()
    ro1.mid()
    ra1[2].fin()
    rb1[2].fin()
    ra2.start()
    rb2.start()
    for k in (1, -1):
        ra1[k].fin()
        rb1[k].fin()
    ra2.mid()
    rb2.mid()
    ro1.fin()
    own = PO[x].astype(F32)
    for k in range(4):
        PS[k] = own[4 * k:4 * k + 4]
    ro2.start()
    ra1[0].fin()
    rb1[0].fin()
    ro2.mid()
    ra2.fin()
    rb2.fin()
    ro2.fin()

    for n in range(4):
        at = lanes(n, 768)
        whole = Pb[here, :, at].astype(F32)
        for s in range(4):
            rzs[s, :, at] = whole[8 * s:8 * s + 8].astype(BF16)
    for s in range(4):
        rzos[s] = PS[y, s:s + 1, :]
    rid = [(new_id(), new_id()) for _ in range(3)]
    for k in (1, 3, 2):
        to = near(z, k)
        send(rzs.at[to], rzr.at[z], rid[k - 1][0], (c, chip(dz=k)))
        send(rzos.at[to], rzor.at[z], rid[k - 1][1], (c, chip(dz=k)))
    rzr[z] = rzs[z]
    rzor[z] = rzos[z]
    for k in (1, 3, 2):
        frm = near(z, -k)
        take(rzr.at[frm], rid[k - 1][0], (c, chip(dz=k)))
        take(rzor.at[frm], rid[k - 1][1], (c, chip(dz=k)))

    take0 = pick0[:, 0:48].astype(BF16)
    take1 = pick1[:, 0:48].astype(BF16)
    for n in range(4):
        at = lanes(n, 768)
        rows = jnp.concatenate(
            [rzr[e, :, at].astype(F32) for e in range(4)]
            + [rzor[e, :, at] for e in range(4)]
            + [jnp.zeros((12, 768), F32)],
            axis=0,
        ).astype(BF16)
        first = jnp.dot(take0, rows, preferred_element_type=F32)
        second = jnp.dot(take1, rows, preferred_element_type=F32)
        layer = (hb[:, at].astype(F32) + w0 * first + w1 * second).astype(out.dtype)
        layer = layer.astype(F32)
        for r in range(4):
            out[r, :, at] = layer[4 * r:4 * r + 4].astype(out.dtype)

    for copy in sent:
        copy.wait_send()


def shards(
    queries, cache_keys, cache_values, lengths, new_keys, new_values, residual, norm_gain,
    expert_ids, gate_logits, w_gate, w_up, w_down,
):
    hbm = pl.BlockSpec(memory_space=pl.ANY)
    vmem = pl.BlockSpec(memory_space=pltpu.VMEM)
    smem = pl.BlockSpec(memory_space=pltpu.SMEM)
    V = pltpu.VMEM
    rows = sum(32 * len(g) for g in GROUPS) + 64
    return pl.pallas_call(
        kernel,
        out_shape=jax.ShapeDtypeStruct((4, 4, HALF), BF16),
        in_specs=[smem, hbm, hbm, hbm, hbm, hbm, hbm, vmem, vmem, vmem, hbm, hbm, hbm],
        out_specs=vmem,
        scratch_shapes=[
            V((4, 4, HALF), BF16), V((4, 128, 512), BF16), V((4, 128, 512), BF16),
            V((4, 4, 512), BF16), V((4, 4, 512), BF16), V((4, 4, HALF), BF16),
            V((16, HALF), BF16), V((16, HALF), BF16), V((16, 128), F32), V((16, 128), F32),
            V((4, 8, HALF), BF16), V((4, 8, HALF), BF16), V((4, 1, HALF), F32), V((4, 1, HALF), F32),
            V((16, 32, HALF), BF16), V((4, 4, HALF), F32), V((4, 16, HALF), BF16),
            V((HALF, 2 * FF), BF16), V((FF, HALF), BF16),
            V((rows, 2 * FF), F32), V((rows, 2 * FF), BF16), V((rows, 2 * FF), BF16), V((rows, FF), BF16),
            V((16, 32, HALF), BF16), V((4, 16, HALF), BF16), V((4, 4, HALF), F32),
            V((4, 2, 32, 768), BF16), V((4, 2, 32, FA), BF16), V((2, 32, 768), BF16), V((2, 32, FA), BF16),
            V((4, 2, 32, 896), BF16), V((4, 2, 32, FB), BF16), V((2, 32, 896), BF16), V((2, 32, FB), BF16),
            V((2, 16, 1536), BF16), V((2, 16, HALF), BF16), V((2, 4, 1536), F32), V((2, 4, HALF), F32),
            V((4, 8, HALF), BF16), V((4, 8, HALF), BF16), V((4, 1, HALF), F32), V((4, 1, HALF), F32),
            pltpu.SemaphoreType.DMA((9,)), pltpu.SemaphoreType.DMA((NSEM,)), pltpu.SemaphoreType.DMA((NSEM,)),
        ],
        compiler_params=pltpu.CompilerParams(collective_id=0, has_side_effects=True),
        name="layer",
    )(
        lengths, queries, cache_keys, cache_values, new_keys, new_values, residual,
        norm_gain.reshape(48, 128), expert_ids, gate_logits, w_gate, w_up, w_down,
    )


def solution(mesh):
    return jax.shard_map(
        shards,
        mesh=mesh,
        in_specs=(
            P("dev", None, None),
            P("dev", None, None),
            P("dev", None, None),
            P("dev"),
            P("dev", None, None),
            P("dev", None, None),
            P("dev", None, None),
            P(),
            P("dev", None),
            P("dev", None),
            P(None, "dev"),
            P(None, "dev"),
            P("dev", None),
        ),
        out_specs=P("dev", None, "sec"),
        check_vma=False,
    )
```

```python
import jax
import jax.numpy as jnp
from jax import lax
from jax.experimental import pallas as pl
from jax.experimental.pallas import tpu as pltpu
from jax.sharding import PartitionSpec as P

HD = 128
EPS = 1e-05

F32 = jnp.float32
BF16 = jnp.bfloat16
HALF = 3072
FF = 512
NSEM = 288
TILE = 256
WAVES = 2
FA = (1536, 1280)
CUT_A = (768, 640)
CUT_B = (768, 896)
ORDER = (0, 1, -1, 2)
BLOCKS = tuple((i, j) for i in range(4) for j in range(4))


def lanes(j, n=128):
    return slice(j * n, (j + 1) * n)


def kernel(
    lens, q_hbm, k_hbm, v_hbm, nk_hbm, nv_hbm, res_hbm, gain, ids, logits, wg_hbm, wu_hbm, wd_hbm,
    out,
    qb, kb, vb, nkb, nvb, resb, hb, xn, ssb, ssr,
    zs, zr, zos, zor, X, XOs, XO, W, Wd, GU, GUs, GUr, H, Pb, PO, PS,
    ad, af, ad2, af2, bd, bf, bd2, bf2, od, of, od2, of2, rzs, rzr, rzos, rzor,
    lsem, ssem, rsem,
):
    c = lax.axis_index("sec")
    d = lax.axis_index("dev")
    z = d // 16
    x = (d // 4) % 4
    y = d % 4
    here = x * 4 + y

    def near(v, by):
        return lax.rem(v + (by % 4), 4)

    def chip(dz=0, dx=0, dy=0):
        return near(z, dz) * 16 + near(x, dx) * 4 + near(y, dy)

    steps = {"x": lambda by: (c, chip(dx=by)), "y": lambda by: (c, chip(dy=by))}
    zpeers = [(c, chip(dz=k)) for k in (1, 2, 3)]
    sibling = (1 - c, d)
    partners = zpeers + [sibling] + [steps[a](by) for a in ("x", "y") for by in (1, -1)]

    barrier = pltpu.get_barrier_semaphore()
    for p in partners:
        pl.semaphore_signal(barrier, inc=1, device_id=p, device_id_type=pl.DeviceIdType.MESH)

    feats = pl.ds(pl.multiple_of(c * HALF, HALF), HALF)
    kvs = pl.ds(pl.multiple_of(c * 512, 512), 512)
    local = []
    for i, (src, dst) in enumerate((
        (q_hbm.at[:, :, feats], qb),
        (k_hbm.at[:, :, kvs], kb),
        (nk_hbm.at[:, :, kvs], nkb),
        (v_hbm.at[:, :, kvs], vb),
        (nv_hbm.at[:, :, kvs], nvb),
        (res_hbm.at[:, :, feats], resb),
        (wg_hbm.at[feats, :], W.at[:, pl.ds(0, FF)]),
        (wu_hbm.at[feats, :], W.at[:, pl.ds(FF, FF)]),
        (wd_hbm.at[:, feats], Wd),
    )):
        copy = pltpu.make_async_copy(src, dst, lsem.at[i])
        copy.start()
        local.append(copy)

    counter = [0]
    sent = []

    def new_id():
        counter[0] += 1
        return counter[0] - 1

    def send(src, dst, sem, dev):
        copy = pltpu.make_async_remote_copy(
            src_ref=src, dst_ref=dst, send_sem=ssem.at[sem], recv_sem=rsem.at[sem],
            device_id=dev, device_id_type=pl.DeviceIdType.MESH,
        )
        copy.start()
        sent.append(copy)

    def take(dst, sem, dev):
        pltpu.make_async_remote_copy(
            src_ref=dst, dst_ref=dst, send_sem=ssem.at[sem], recv_sem=rsem.at[sem],
            device_id=dev, device_id_type=pl.DeviceIdType.MESH,
        ).wait_recv()

    square = (16, 16)
    down_row = lax.broadcasted_iota(jnp.int32, square, 0)
    across = lax.broadcasted_iota(jnp.int32, square, 1)

    def column(ref, k):
        rows = jnp.broadcast_to(ref[k:k + 1, :], square)
        return jnp.sum(jnp.where(down_row == across, rows, jnp.zeros_like(rows)), axis=1, keepdims=True)

    id0, id1 = column(ids, 0), column(ids, 1)
    slot = lax.broadcasted_iota(jnp.int32, (16, 128), 1)
    who = jnp.where(slot < 32, slot // 8, slot - 32)
    rank = jnp.where(slot < 32, slot % 8, 8)
    hit0 = id0 == who
    hit1 = id1 == who
    hit = jnp.where(hit0 | hit1, 1.0, 0.0)
    before = jnp.where(across < down_row, 1.0, 0.0)
    ahead = jnp.dot(before.astype(BF16), hit.astype(BF16), preferred_element_type=F32)
    chosen = ahead == rank.astype(F32)
    pick0 = jnp.where(hit0 & chosen, 1.0, 0.0)
    pick1 = jnp.where(hit1 & chosen, 1.0, 0.0)
    packing = jnp.transpose(pick0 + pick1)[0:48].astype(BF16)
    l0, l1 = column(logits, 0), column(logits, 1)
    top = jnp.maximum(l0, l1)
    e0, e1 = jnp.exp(l0 - top), jnp.exp(l1 - top)
    w0 = e0 / (e0 + e1)
    w1 = e1 / (e0 + e1)

    for copy in local[:6]:
        copy.wait()
    row = lax.broadcasted_iota(jnp.int32, (96, 128), 0)
    col = lax.broadcasted_iota(jnp.int32, (96, 128), 1)
    lenv = jnp.concatenate([jnp.full((24, 128), lens[r], jnp.int32) for r in range(4)], axis=0)
    in_cache = col < lenv
    row16 = lax.broadcasted_iota(jnp.int32, (96, 16), 0)
    col16 = lax.broadcasted_iota(jnp.int32, (96, 16), 1)
    in_window = (row16 // 24 == col16 // 4) & (col16 % 4 <= row16 % 4)
    scale = HD ** (-0.5)
    ss = jnp.zeros((16, 128), F32)
    contract = (((1,), (1,)), ((), ()))
    for g in range(4):
        qs = [
            jnp.concatenate([qb[r, :, lanes(g * 6 + h)].astype(F32) for h in range(6)], axis=0)
            for r in range(4)
        ]
        sc = jnp.concatenate([
            lax.dot_general(qs[r].astype(BF16), kb[r, :, lanes(g)], contract, preferred_element_type=F32)
            for r in range(4)
        ], axis=0) * scale
        nk = jnp.concatenate([nkb[r, :, lanes(g)].astype(F32) for r in range(4)], axis=0).astype(BF16)
        nv = jnp.concatenate([nvb[r, :, lanes(g)].astype(F32) for r in range(4)], axis=0).astype(BF16)
        qa = jnp.concatenate(qs, axis=0).astype(BF16)
        sn = lax.dot_general(qa, nk, contract, preferred_element_type=F32) * scale
        sc = jnp.where(in_cache, sc, -1e30)
        sn = jnp.where(in_window, sn, -1e30)
        peak = jnp.maximum(jnp.max(sc, axis=1, keepdims=True), jnp.max(sn, axis=1, keepdims=True))
        ec = jnp.exp(sc - peak)
        en = jnp.exp(sn - peak)
        total = jnp.sum(ec, axis=1, keepdims=True) + jnp.sum(en, axis=1, keepdims=True)
        inv = 1.0 / total
        pc = ec * inv
        pn = (en * inv).astype(BF16)
        att = jnp.concatenate([
            jnp.dot(pc[24 * r:24 * r + 24].astype(BF16), vb[r, :, lanes(g)], preferred_element_type=F32)
            for r in range(4)
        ], axis=0) + jnp.dot(pn, nv, preferred_element_type=F32)
        for h in range(6):
            j = g * 6 + h
            part = jnp.concatenate([att[r * 24 + h * 4:r * 24 + h * 4 + 4] for r in range(4)], axis=0)
            res = jnp.concatenate([resb[r, :, lanes(j)].astype(F32) for r in range(4)], axis=0)
            hst = (res + part).astype(BF16)
            hb[:, lanes(j)] = hst
            hf = hst.astype(F32)
            ss = ss + hf * hf
    ssb[...] = jnp.broadcast_to(jnp.sum(ss, axis=1, keepdims=True), (16, 128))
    pl.semaphore_wait(barrier, len(partners))
    sid = new_id()
    send(ssb, ssr, sid, sibling)

    take(ssr, sid, sibling)
    inv = lax.rsqrt((ssb[...] + ssr[...]) / (2 * HALF) + EPS)
    gains = gain[pl.ds(pl.multiple_of(c * 24, 8), 24), :]
    for j in range(24):
        xn[:, lanes(j)] = (hb[:, lanes(j)].astype(F32) * inv * gains[j:j + 1]).astype(BF16)
    for n in range(4):
        at = lanes(n, 768)
        packed = jnp.dot(packing, xn[:, at], preferred_element_type=F32)
        for e in range(4):
            zs[e, :, at] = packed[8 * e:8 * e + 8].astype(BF16)
            zos[e, :, at] = packed[32 + e:33 + e]

    zid = {k: (new_id(), new_id()) for k in (1, 3, 2)}
    for k in (1, 3, 2):
        send(zs.at[near(z, k)], zr.at[k], zid[k][0], (c, chip(dz=k)))
    for k in (1, 3, 2):
        send(zos.at[near(z, k)], zor.at[k], zid[k][1], (c, chip(dz=k)))

    def form(w, first, second):
        for n in range(4):
            at = lanes(n, 768)
            X[w, here, :, at] = jnp.concatenate([first(at).astype(F32), second(at).astype(F32)], axis=0).astype(BF16)

    take(zr.at[1], zid[1][0], (c, chip(dz=1)))
    form(0, lambda at: zs[z, :, at], lambda at: zr[1, :, at])

    def second_wave():
        for k in (3, 2):
            take(zr.at[k], zid[k][0], (c, chip(dz=k)))
        form(1, lambda at: zr[3, :, at], lambda at: zr[2, :, at])
        for k in (1, 3, 2):
            take(zor.at[k], zid[k][1], (c, chip(dz=k)))
        XOs[y, 0:1, :] = zos[z]
        for k in (1, 2, 3):
            XOs[y, k:k + 1, :] = zor[k]

    def blk(dx, dy):
        return near(x, dx) * 4 + near(y, dy)

    class Gather:
        def __init__(self, axis, view, size, cut):
            self.one = lambda r: view(r, 0, cut)
            self.two = lambda r: view(r, cut, size - cut)
            self.dev = {by: steps[axis](by) for by in (1, -1)}
            self.id = [new_id() for _ in range(6)]

        def start(self):
            one, two = self.one(0), self.two(0)
            send(one, one, self.id[0], self.dev[1])
            send(two, two, self.id[1], self.dev[-1])
            send(two, two, self.id[2], self.dev[1])
            send(one, one, self.id[3], self.dev[-1])

        def pass_on(self):
            v = self.one(-1)
            take(v, self.id[0], self.dev[1])
            send(v, v, self.id[4], self.dev[1])
            v = self.two(1)
            take(v, self.id[1], self.dev[-1])
            send(v, v, self.id[5], self.dev[-1])

        def rest(self):
            take(self.two(-1), self.id[2], self.dev[1])
            take(self.one(1), self.id[3], self.dev[-1])

        def far(self):
            take(self.one(2), self.id[4], self.dev[1])
            take(self.two(2), self.id[5], self.dev[-1])

    def gathers(w):
        fa, ca, cb = FA[w], CUT_A[w], CUT_B[w]
        fb = HALF - fa
        Xw = X.at[w]
        a1 = Gather("y", lambda r, lo, n: Xw.at[blk(0, r), :, pl.ds(lo, n)], fa, ca)
        b1 = Gather("x", lambda r, lo, n: Xw.at[blk(r, 0), :, pl.ds(fa + lo, n)], fb, cb)
        a2 = {
            k: Gather("x", lambda r, lo, n, k=k: Xw.at[blk(r, k), :, pl.ds(lo, n)], fa, ca) for k in ORDER
        }
        b2 = {
            k: Gather("y", lambda r, lo, n, k=k: Xw.at[blk(k, r), :, pl.ds(fa + lo, n)], fb, cb) for k in ORDER
        }
        if w == 1:
            o1 = Gather("y", lambda r, lo, n: XOs.at[near(y, r), :, pl.ds(lo, n)], HALF, HALF // 2)
            o2 = Gather("x", lambda r, lo, n: XO.at[near(x, r), :, pl.ds(lo, n)], HALF, HALF // 2)

        def start():
            a1.start()
            b1.start()
            if w == 1:
                o1.start()
            a2[0].start()
            b2[0].start()

        def line():
            a1.pass_on()
            b1.pass_on()
            a1.rest()
            a2[1].start()
            b1.rest()
            b2[1].start()
            a2[-1].start()
            b2[-1].start()

        def line_over():
            o1.pass_on()
            o1.rest()

        def own():
            a2[0].pass_on()
            b2[0].pass_on()

        def far_line():
            a1.far()
            a2[2].start()
            b1.far()
            b2[2].start()

        def over():
            o1.far()
            XO[x] = jnp.concatenate([XOs[k] for k in range(4)], axis=0).astype(BF16)
            o2.start()

        def sides(k):
            a2[k].pass_on()
            b2[k].pass_on()

        def over_pass():
            o2.pass_on()

        def finish():
            for k in ORDER:
                a2[k].rest()
                b2[k].rest()
                a2[k].far()
                b2[k].far()
            if w == 1:
                o2.rest()
                o2.far()

        steps_of = [start, line, own, far_line, lambda: sides(1), lambda: sides(-1), lambda: sides(2), finish]
        if w == 1:
            steps_of = [
                start, line, line_over, own, far_line, over, lambda: sides(1), lambda: sides(-1), lambda: sides(2),
                over_pass, finish,
            ]
        return steps_of

    place = ((0, 256), (256, 320))
    gid = [[[new_id(), new_id()] for _ in range(2)] for _ in range(WAVES)]

    def experts(w):
        lo, size = place[w]
        v = pl.ds(lo, size)

        def rows():
            parts = [X[w, k] for k in range(16)]
            if w == 1:
                parts += [XO[k] for k in range(4)]
            return jnp.concatenate(parts, axis=0)

        def up(t):
            cols = pl.ds(t * TILE, TILE)
            acc = jnp.dot(rows(), W[:, cols], preferred_element_type=F32)
            GU[v, cols] = acc
            GUs[v, cols] = acc.astype(BF16)

        def up_half(h):
            up(h)
            up(h + 2)
            for i, t in enumerate((h, h + 2)):
                cols = pl.ds(t * TILE, TILE)
                send(GUs.at[v, cols], GUr.at[v, cols], gid[w][h][i], sibling)

        def hidden(h):
            for i, t in enumerate((h, h + 2)):
                take(GUr.at[v, pl.ds(t * TILE, TILE)], gid[w][h][i], sibling)
            one = pl.ds(h * TILE, TILE)
            two = pl.ds(FF + h * TILE, TILE)

            @pl.loop(0, size // 32)
            def _(i):
                r = pl.ds(pl.multiple_of(lo + i * 32, 32), 32)
                gate = GU[r, one] + GUr[r, one].astype(F32)
                upward = GU[r, two] + GUr[r, two].astype(F32)
                H[r, one] = (jax.nn.silu(gate) * upward).astype(BF16)

        def down(t):
            cols = pl.ds(t * TILE, TILE)
            acc = jnp.dot(H[v, :], Wd[:, cols], preferred_element_type=F32).astype(BF16)
            for k in range(16):
                Pb[w, k, :, cols] = acc[16 * k:16 * k + 16]
            if w == 1:
                for k in range(4):
                    PO[k, :, cols] = acc[256 + 16 * k:272 + 16 * k]

        return (
            [lambda: up_half(0), lambda: up_half(1), lambda: hidden(0), lambda: hidden(1)]
            + [lambda t=t: (down(2 * t), down(2 * t + 1)) for t in range(6)]
        )

    def add_into(dst, srcs):
        n = dst.shape[-1]
        for j in range(n // 128):
            s = pl.ds(j * 128, 128)
            acc = dst[:, s].astype(F32)
            for src in srcs:
                acc = acc + src[:, s].astype(F32)
            dst[:, s] = acc.astype(dst.dtype)

    class Scatter:
        def __init__(self, axis, view, size, cut, dbuf, fbuf):
            self.one = lambda r: view(r, 0, cut)
            self.two = lambda r: view(r, cut, size - cut)
            self.whole = lambda r: view(r, 0, size)
            self.dev = {by: steps[axis](by) for by in (1, -1)}
            self.id = [new_id() for _ in range(6)]
            self.d = (dbuf(0).at[:, pl.ds(0, cut)], dbuf(1).at[:, pl.ds(0, size - cut)])
            self.f = (fbuf(0), fbuf(1))
            self.f1 = [f.at[:, pl.ds(0, cut)] for f in self.f]
            self.f2 = [f.at[:, pl.ds(cut, size - cut)] for f in self.f]

        def start(self):
            send(self.one(2), self.d[0], self.id[0], self.dev[1])
            send(self.two(2), self.d[1], self.id[1], self.dev[-1])

        def plain(self):
            send(self.two(1), self.f2[0], self.id[2], self.dev[1])
            send(self.one(-1), self.f1[1], self.id[3], self.dev[-1])

        def mid(self):
            take(self.d[0], self.id[0], self.dev[1])
            add_into(self.one(1), [self.d[0]])
            send(self.one(1), self.f1[0], self.id[4], self.dev[1])
            take(self.d[1], self.id[1], self.dev[-1])
            add_into(self.two(-1), [self.d[1]])
            send(self.two(-1), self.f2[1], self.id[5], self.dev[-1])

        def fin(self):
            take(self.f2[0], self.id[2], self.dev[1])
            take(self.f1[1], self.id[3], self.dev[-1])
            take(self.f1[0], self.id[4], self.dev[1])
            take(self.f2[1], self.id[5], self.dev[-1])
            add_into(self.whole(0), self.f)

    rid = {k: (new_id(), new_id()) for k in (1, 2, 3)}

    def scatters(w):
        fa, ca, cb = FA[w], CUT_A[w], CUT_B[w]
        fb = HALF - fa
        Pw = Pb.at[w]
        wa, wb = pl.ds(0, fa), pl.ds(0, fb)
        a1, b1 = {}, {}
        for i, k in enumerate(ORDER):
            a1[k] = Scatter(
                "x", lambda r, lo, n, k=k: Pw.at[blk(r, k), :, pl.ds(lo, n)], fa, ca,
                lambda s, i=i: ad.at[w, i, s], lambda s, i=i: af.at[w, i, s, :, wa],
            )
            b1[k] = Scatter(
                "y", lambda r, lo, n, k=k: Pw.at[blk(k, r), :, pl.ds(fa + lo, n)], fb, cb,
                lambda s, i=i: bd.at[w, i, s], lambda s, i=i: bf.at[w, i, s, :, wb],
            )
        a2 = Scatter(
            "y", lambda r, lo, n: Pw.at[blk(0, r), :, pl.ds(lo, n)], fa, ca,
            lambda s: ad2.at[w, s], lambda s: af2.at[w, s, :, wa],
        )
        b2 = Scatter(
            "x", lambda r, lo, n: Pw.at[blk(r, 0), :, pl.ds(fa + lo, n)], fb, cb,
            lambda s: bd2.at[w, s], lambda s: bf2.at[w, s, :, wb],
        )
        if w == 1:
            o1 = Scatter(
                "x", lambda r, lo, n: PO.at[near(x, r), :, pl.ds(lo, n)], HALF, HALF // 2,
                lambda s: od.at[s], lambda s: of.at[s],
            )
            o2 = Scatter(
                "y", lambda r, lo, n: PS.at[near(y, r), :, pl.ds(lo, n)], HALF, HALF // 2,
                lambda s: od2.at[s], lambda s: of2.at[s],
            )
        back = (2, 1, -1, 0)

        def start():
            if w == 1:
                o1.start()
            for k in back:
                a1[k].start()
                b1[k].start()
            if w == 1:
                o1.plain()
            for k in back:
                a1[k].plain()
                b1[k].plain()

        def over_mid():
            o1.mid()

        def mid(k):
            a1[k].mid()
            b1[k].mid()

        def far():
            a1[2].fin()
            a2.start()
            b1[2].fin()
            b2.start()

        def over():
            o1.fin()
            own = PO[x].astype(F32)
            for k in range(4):
                PS[k] = own[4 * k:4 * k + 4]
            o2.start()
            o2.plain()

        def sides():
            for k in (1, -1):
                a1[k].fin()
                b1[k].fin()
            a2.plain()
            b2.plain()

        def cross():
            a2.mid()
            b2.mid()

        def over_cross():
            o2.mid()

        def finish():
            a1[0].fin()
            b1[0].fin()
            a2.fin()
            b2.fin()
            if w == 1:
                o2.fin()

        def home():
            for n in range(4):
                at = lanes(n, 768)
                whole = Pw[here, :, at].astype(F32)
                rzs[w, 0, :, at] = whole[0:8].astype(BF16)
                rzs[w, 1, :, at] = whole[8:16].astype(BF16)
            if w == 0:
                send(rzs.at[0, 1], rzr.at[3], rid[3][0], (c, chip(dz=-1)))
            else:
                send(rzs.at[1, 1], rzr.at[2], rid[2][0], (c, chip(dz=2)))
                send(rzs.at[1, 0], rzr.at[1], rid[1][0], (c, chip(dz=1)))
                for s in range(4):
                    rzos[s] = PS[y, s:s + 1, :]
                for s, k in ((2, 2), (1, 3), (3, 1)):
                    send(rzos.at[s], rzor.at[k], rid[k][1], (c, chip(dz=k)))

        if w == 0:
            return [start] + [lambda k=k: mid(k) for k in back] + [far, sides, cross, finish, home]
        return (
            [start, over_mid] + [lambda k=k: mid(k) for k in back]
            + [over, far, sides, over_cross, cross, finish, home]
        )

    g0, g1 = gathers(0), gathers(1)
    x0, x1 = experts(0), experts(1)
    s0, s1 = scatters(0), scatters(1)

    def run(*todo):
        for f in todo:
            f()

    run(*g0[:4])
    second_wave()
    run(*g0[4:6])
    run(g1[0])
    run(*g0[6:])
    for copy in local[6:]:
        copy.wait()
    run(g1[1], x0[0], g1[2], g1[3], x0[1], g1[4], g1[5], x0[2], x0[3], g1[6])
    run(x0[4], x0[5], g1[7], x0[6], x0[7], g1[8], x0[8], x0[9])
    run(g1[9], s0[0], g1[10])
    run(x1[0], s0[1], s0[2], x1[1], s0[3], s0[4], x1[2], x1[3], s0[5], s0[6])
    run(x1[4], x1[5], s0[7], x1[6], x1[7], x1[8], x1[9])
    run(s1[0], s0[8], s0[9])
    run(*s1[1:])

    rzr[0] = rzs[0, 0]
    rzor[0] = rzos[0]
    for k in (3, 1, 2):
        take(rzr.at[k], rid[k][0], (c, chip(dz=k)))
        take(rzor.at[k], rid[k][1], (c, chip(dz=k)))
    take0 = pick0[:, 0:48].astype(BF16)
    take1 = pick1[:, 0:48].astype(BF16)
    behind = [lax.rem(z - e + 4, 4) for e in range(4)]
    for n in range(4):
        at = lanes(n, 768)
        rows = jnp.concatenate(
            [rzr[behind[e], :, at].astype(F32) for e in range(4)]
            + [rzor[behind[e], :, at] for e in range(4)]
            + [jnp.zeros((12, 768), F32)],
            axis=0,
        ).astype(BF16)
        first = jnp.dot(take0, rows, preferred_element_type=F32)
        second = jnp.dot(take1, rows, preferred_element_type=F32)
        layer = hb[:, at].astype(F32) + w0 * first + w1 * second
        for r in range(4):
            out[r, :, at] = layer[4 * r:4 * r + 4].astype(out.dtype)

    assert counter[0] <= NSEM
    for copy in sent:
        copy.wait_send()


def shards(
    queries, cache_keys, cache_values, lengths, new_keys, new_values, residual, norm_gain,
    expert_ids, gate_logits, w_gate, w_up, w_down,
):
    hbm = pl.BlockSpec(memory_space=pl.ANY)
    vmem = pl.BlockSpec(memory_space=pltpu.VMEM)
    smem = pl.BlockSpec(memory_space=pltpu.SMEM)
    V = pltpu.VMEM
    rows = 576
    return pl.pallas_call(
        kernel,
        out_shape=jax.ShapeDtypeStruct((4, 4, HALF), BF16),
        in_specs=[smem, hbm, hbm, hbm, hbm, hbm, hbm, vmem, vmem, vmem, hbm, hbm, hbm],
        out_specs=vmem,
        scratch_shapes=[
            V((4, 4, HALF), BF16), V((4, 128, 512), BF16), V((4, 128, 512), BF16),
            V((4, 4, 512), BF16), V((4, 4, 512), BF16), V((4, 4, HALF), BF16),
            V((16, HALF), BF16), V((16, HALF), BF16), V((16, 128), F32), V((16, 128), F32),
            V((4, 8, HALF), BF16), V((4, 8, HALF), BF16), V((4, 1, HALF), F32), V((4, 1, HALF), F32),
            V((WAVES, 16, 16, HALF), BF16), V((4, 4, HALF), F32), V((4, 16, HALF), BF16),
            V((HALF, 2 * FF), BF16), V((FF, HALF), BF16),
            V((rows, 2 * FF), F32), V((rows, 2 * FF), BF16), V((rows, 2 * FF), BF16), V((rows, FF), BF16),
            V((WAVES, 16, 16, HALF), BF16), V((4, 16, HALF), BF16), V((4, 4, HALF), F32),
            V((WAVES, 4, 2, 16, 768), BF16), V((WAVES, 4, 2, 16, 1536), BF16),
            V((WAVES, 2, 16, 768), BF16), V((WAVES, 2, 16, 1536), BF16),
            V((WAVES, 4, 2, 16, 896), BF16), V((WAVES, 4, 2, 16, 1792), BF16),
            V((WAVES, 2, 16, 896), BF16), V((WAVES, 2, 16, 1792), BF16),
            V((2, 16, 1536), BF16), V((2, 16, HALF), BF16), V((2, 4, 1536), F32), V((2, 4, HALF), F32),
            V((WAVES, 2, 8, HALF), BF16), V((4, 8, HALF), BF16), V((4, 1, HALF), F32), V((4, 1, HALF), F32),
            pltpu.SemaphoreType.DMA((9,)), pltpu.SemaphoreType.DMA((NSEM,)), pltpu.SemaphoreType.DMA((NSEM,)),
        ],
        compiler_params=pltpu.CompilerParams(collective_id=0, has_side_effects=True),
        name="layer",
    )(
        lengths, queries, cache_keys, cache_values, new_keys, new_values, residual,
        norm_gain.reshape(48, 128), expert_ids.T, gate_logits.T, w_gate, w_up, w_down,
    )


def solution(mesh):
    return jax.shard_map(
        shards,
        mesh=mesh,
        in_specs=(
            P("dev", None, None),
            P("dev", None, None),
            P("dev", None, None),
            P("dev"),
            P("dev", None, None),
            P("dev", None, None),
            P("dev", None, None),
            P(),
            P("dev", None),
            P("dev", None),
            P(None, "dev"),
            P(None, "dev"),
            P("dev", None),
        ),
        out_specs=P("dev", None, "sec"),
        check_vma=False,
    )
```

```python
import jax
import jax.numpy as jnp
from jax import lax
from jax.experimental import pallas as pl
from jax.experimental.pallas import tpu as pltpu
from jax.sharding import PartitionSpec as P

HD = 128
EPS = 1e-05

F32 = jnp.float32
BF16 = jnp.bfloat16
HALF = 3072
FF = 512
NSEM = 288
TILE = 256
WAVES = 2
FA = (1536, 1280)
CUT_A = (768, 640)
CUT_B = (768, 896)
ORDER = (0, 1, -1, 2)
BLOCKS = tuple((i, j) for i in range(4) for j in range(4))


def lanes(j, n=128):
    return slice(j * n, (j + 1) * n)


def kernel(
    lens, q_hbm, k_hbm, v_hbm, nk_hbm, nv_hbm, res_hbm, gain, ids, logits, wg_hbm, wu_hbm, wd_hbm,
    out,
    ob, qb, kb, vb, nkb, nvb, resb, hb, xn, ssb, ssr,
    zs, zr, zos, zor, X, XOs, XO, W, Wd, GU, GUs, GUr, H, Pb, PO, PS,
    ad, af, ad2, af2, bd, bf, bd2, bf2, od, of, od2, of2, rzs, rzr, rzos, rzor,
    lsem, ssem, rsem,
):
    c = lax.axis_index("sec")
    d = lax.axis_index("dev")
    z = d // 16
    x = (d // 4) % 4
    y = d % 4
    here = x * 4 + y

    def near(v, by):
        return lax.rem(v + (by % 4), 4)

    def chip(dz=0, dx=0, dy=0):
        return near(z, dz) * 16 + near(x, dx) * 4 + near(y, dy)

    steps = {"x": lambda by: (c, chip(dx=by)), "y": lambda by: (c, chip(dy=by))}
    zpeers = [(c, chip(dz=k)) for k in (1, 2, 3)]
    sibling = (1 - c, d)
    partners = zpeers + [sibling] + [steps[a](by) for a in ("x", "y") for by in (1, -1)]

    barrier = pltpu.get_barrier_semaphore()
    for p in partners:
        pl.semaphore_signal(barrier, inc=1, device_id=p, device_id_type=pl.DeviceIdType.MESH)

    feats = pl.ds(pl.multiple_of(c * HALF, HALF), HALF)
    kvs = pl.ds(pl.multiple_of(c * 512, 512), 512)
    local = []
    for i, (src, dst) in enumerate((
        (q_hbm.at[:, :, feats], qb),
        (k_hbm.at[:, :, kvs], kb),
        (nk_hbm.at[:, :, kvs], nkb),
        (v_hbm.at[:, :, kvs], vb),
        (nv_hbm.at[:, :, kvs], nvb),
        (res_hbm.at[:, :, feats], resb),
        (wg_hbm.at[feats, :], W.at[:, pl.ds(0, FF)]),
        (wu_hbm.at[feats, :], W.at[:, pl.ds(FF, FF)]),
        (wd_hbm.at[:, feats], Wd),
    )):
        copy = pltpu.make_async_copy(src, dst, lsem.at[i])
        if i < 6:
            copy.start()
        local.append(copy)

    counter = [0]
    sent = []
    flushed = [0]

    def new_id():
        counter[0] += 1
        return counter[0] - 1

    def send(src, dst, sem, dev):
        copy = pltpu.make_async_remote_copy(
            src_ref=src, dst_ref=dst, send_sem=ssem.at[sem], recv_sem=rsem.at[sem],
            device_id=dev, device_id_type=pl.DeviceIdType.MESH,
        )
        copy.start()
        sent.append(copy)

    def flush(upto):
        for copy in sent[flushed[0]:upto]:
            copy.wait_send()
        flushed[0] = max(flushed[0], upto)

    def take(dst, sem, dev):
        pltpu.make_async_remote_copy(
            src_ref=dst, dst_ref=dst, send_sem=ssem.at[sem], recv_sem=rsem.at[sem],
            device_id=dev, device_id_type=pl.DeviceIdType.MESH,
        ).wait_recv()

    square = (16, 16)
    down_row = lax.broadcasted_iota(jnp.int32, square, 0)
    across = lax.broadcasted_iota(jnp.int32, square, 1)

    def column(ref, k):
        rows = jnp.broadcast_to(ref[k:k + 1, :], square)
        return jnp.sum(jnp.where(down_row == across, rows, jnp.zeros_like(rows)), axis=1, keepdims=True)

    id0, id1 = column(ids, 0), column(ids, 1)
    slot = lax.broadcasted_iota(jnp.int32, (16, 128), 1)
    who = jnp.where(slot < 32, slot // 8, slot - 32)
    rank = jnp.where(slot < 32, slot % 8, 8)
    hit0 = id0 == who
    hit1 = id1 == who
    hit = jnp.where(hit0 | hit1, 1.0, 0.0)
    before = jnp.where(across < down_row, 1.0, 0.0)
    ahead = jnp.dot(before.astype(BF16), hit.astype(BF16), preferred_element_type=F32)
    chosen = ahead == rank.astype(F32)
    pick0 = jnp.where(hit0 & chosen, 1.0, 0.0)
    pick1 = jnp.where(hit1 & chosen, 1.0, 0.0)
    packing = jnp.transpose(pick0 + pick1)[0:48].astype(BF16)
    l0, l1 = column(logits, 0), column(logits, 1)
    top = jnp.maximum(l0, l1)
    e0, e1 = jnp.exp(l0 - top), jnp.exp(l1 - top)
    w0 = e0 / (e0 + e1)
    w1 = e1 / (e0 + e1)

    for copy in local[:6]:
        copy.wait()
    for copy in local[6:]:
        copy.start()
    row = lax.broadcasted_iota(jnp.int32, (96, 128), 0)
    col = lax.broadcasted_iota(jnp.int32, (96, 128), 1)
    lenv = jnp.concatenate([jnp.full((24, 128), lens[r], jnp.int32) for r in range(4)], axis=0)
    in_cache = col < lenv
    row16 = lax.broadcasted_iota(jnp.int32, (96, 16), 0)
    col16 = lax.broadcasted_iota(jnp.int32, (96, 16), 1)
    in_window = (row16 // 24 == col16 // 4) & (col16 % 4 <= row16 % 4)
    scale = HD ** (-0.5)
    ss = jnp.zeros((16, 128), F32)
    contract = (((1,), (1,)), ((), ()))
    for g in range(4):
        qs = [
            jnp.concatenate([qb[r, :, lanes(g * 6 + h)].astype(F32) for h in range(6)], axis=0)
            for r in range(4)
        ]
        sc = jnp.concatenate([
            lax.dot_general(qs[r].astype(BF16), kb[r, :, lanes(g)], contract, preferred_element_type=F32)
            for r in range(4)
        ], axis=0) * scale
        nk = jnp.concatenate([nkb[r, :, lanes(g)].astype(F32) for r in range(4)], axis=0).astype(BF16)
        nv = jnp.concatenate([nvb[r, :, lanes(g)].astype(F32) for r in range(4)], axis=0).astype(BF16)
        qa = jnp.concatenate(qs, axis=0).astype(BF16)
        sn = lax.dot_general(qa, nk, contract, preferred_element_type=F32) * scale
        sc = jnp.where(in_cache, sc, -1e30)
        sn = jnp.where(in_window, sn, -1e30)
        peak = jnp.maximum(jnp.max(sc, axis=1, keepdims=True), jnp.max(sn, axis=1, keepdims=True))
        ec = jnp.exp(sc - peak)
        en = jnp.exp(sn - peak)
        total = jnp.sum(ec, axis=1, keepdims=True) + jnp.sum(en, axis=1, keepdims=True)
        inv = 1.0 / total
        pc = ec * inv
        pn = (en * inv).astype(BF16)
        att = jnp.concatenate([
            jnp.dot(pc[24 * r:24 * r + 24].astype(BF16), vb[r, :, lanes(g)], preferred_element_type=F32)
            for r in range(4)
        ], axis=0) + jnp.dot(pn, nv, preferred_element_type=F32)
        for h in range(6):
            j = g * 6 + h
            part = jnp.concatenate([att[r * 24 + h * 4:r * 24 + h * 4 + 4] for r in range(4)], axis=0)
            res = jnp.concatenate([resb[r, :, lanes(j)].astype(F32) for r in range(4)], axis=0)
            hst = (res + part).astype(BF16)
            hb[:, lanes(j)] = hst
            hf = hst.astype(F32)
            ss = ss + hf * hf
    ssb[...] = jnp.broadcast_to(jnp.sum(ss, axis=1, keepdims=True), (16, 128))
    pl.semaphore_wait(barrier, len(partners))
    sid = new_id()
    send(ssb, ssr, sid, sibling)

    take(ssr, sid, sibling)
    inv = lax.rsqrt((ssb[...] + ssr[...]) / (2 * HALF) + EPS)
    gains = gain[pl.ds(pl.multiple_of(c * 24, 8), 24), :]
    for j in range(24):
        xn[:, lanes(j)] = (hb[:, lanes(j)].astype(F32) * inv * gains[j:j + 1]).astype(BF16)
    for n in range(4):
        at = lanes(n, 768)
        packed = jnp.dot(packing, xn[:, at], preferred_element_type=F32)
        for e in range(4):
            zs[e, :, at] = packed[8 * e:8 * e + 8].astype(BF16)
            zos[e, :, at] = packed[32 + e:33 + e]

    zid = {k: (new_id(), new_id()) for k in (1, 3, 2)}
    for k in (1, 3, 2):
        send(zs.at[near(z, k)], zr.at[k], zid[k][0], (c, chip(dz=k)))
    for k in (1, 3, 2):
        send(zos.at[near(z, k)], zor.at[k], zid[k][1], (c, chip(dz=k)))

    def form(w, first, second):
        for n in range(4):
            at = lanes(n, 768)
            X[w, here, :, at] = jnp.concatenate([first(at).astype(F32), second(at).astype(F32)], axis=0).astype(BF16)

    take(zr.at[1], zid[1][0], (c, chip(dz=1)))
    form(0, lambda at: zs[z, :, at], lambda at: zr[1, :, at])

    def second_wave():
        for k in (3, 2):
            take(zr.at[k], zid[k][0], (c, chip(dz=k)))
        form(1, lambda at: zr[3, :, at], lambda at: zr[2, :, at])
        for k in (1, 3, 2):
            take(zor.at[k], zid[k][1], (c, chip(dz=k)))
        XOs[y, 0:1, :] = zos[z]
        for k in (1, 2, 3):
            XOs[y, k:k + 1, :] = zor[k]

    def blk(dx, dy):
        return near(x, dx) * 4 + near(y, dy)

    class Gather:
        def __init__(self, axis, view, size, cut):
            self.one = lambda r: view(r, 0, cut)
            self.two = lambda r: view(r, cut, size - cut)
            self.dev = {by: steps[axis](by) for by in (1, -1)}
            self.id = [new_id() for _ in range(6)]

        def start(self):
            one, two = self.one(0), self.two(0)
            send(one, one, self.id[0], self.dev[1])
            send(two, two, self.id[1], self.dev[-1])
            send(two, two, self.id[2], self.dev[1])
            send(one, one, self.id[3], self.dev[-1])

        def pass_on(self):
            v = self.one(-1)
            take(v, self.id[0], self.dev[1])
            send(v, v, self.id[4], self.dev[1])
            v = self.two(1)
            take(v, self.id[1], self.dev[-1])
            send(v, v, self.id[5], self.dev[-1])

        def rest(self):
            take(self.two(-1), self.id[2], self.dev[1])
            take(self.one(1), self.id[3], self.dev[-1])

        def far(self):
            take(self.one(2), self.id[4], self.dev[1])
            take(self.two(2), self.id[5], self.dev[-1])

    def gathers(w):
        fa, ca, cb = FA[w], CUT_A[w], CUT_B[w]
        fb = HALF - fa
        Xw = X.at[w]
        a1 = Gather("y", lambda r, lo, n: Xw.at[blk(0, r), :, pl.ds(lo, n)], fa, ca)
        b1 = Gather("x", lambda r, lo, n: Xw.at[blk(r, 0), :, pl.ds(fa + lo, n)], fb, cb)
        a2 = {
            k: Gather("x", lambda r, lo, n, k=k: Xw.at[blk(r, k), :, pl.ds(lo, n)], fa, ca) for k in ORDER
        }
        b2 = {
            k: Gather("y", lambda r, lo, n, k=k: Xw.at[blk(k, r), :, pl.ds(fa + lo, n)], fb, cb) for k in ORDER
        }
        if w == 1:
            o1 = Gather("y", lambda r, lo, n: XOs.at[near(y, r), :, pl.ds(lo, n)], HALF, HALF // 2)
            o2 = Gather("x", lambda r, lo, n: XO.at[near(x, r), :, pl.ds(lo, n)], HALF, HALF // 2)

        def start():
            a1.start()
            b1.start()
            if w == 1:
                o1.start()
            a2[0].start()
            b2[0].start()

        def line():
            a1.pass_on()
            b1.pass_on()
            a1.rest()
            a2[1].start()
            b1.rest()
            b2[1].start()
            a2[-1].start()
            b2[-1].start()

        def line_over():
            o1.pass_on()
            o1.rest()

        def own():
            a2[0].pass_on()
            b2[0].pass_on()

        def far_line():
            a1.far()
            a2[2].start()
            b1.far()
            b2[2].start()

        def over():
            o1.far()
            XO[x] = jnp.concatenate([XOs[k] for k in range(4)], axis=0).astype(BF16)
            o2.start()

        def sides(k):
            a2[k].pass_on()
            b2[k].pass_on()

        def over_pass():
            o2.pass_on()

        def finish():
            for k in ORDER:
                a2[k].rest()
                b2[k].rest()
                a2[k].far()
                b2[k].far()
            if w == 1:
                o2.rest()
                o2.far()

        steps_of = [start, line, own, far_line, lambda: sides(1), lambda: sides(-1), lambda: sides(2), finish]
        if w == 1:
            steps_of = [
                start, line, line_over, own, far_line, over, lambda: sides(1), lambda: sides(-1), lambda: sides(2),
                over_pass, finish,
            ]
        return steps_of

    place = ((0, 256), (256, 320))
    gid = [[[new_id(), new_id()] for _ in range(2)] for _ in range(WAVES)]

    def experts(w):
        lo, size = place[w]
        v = pl.ds(lo, size)

        def rows():
            parts = [X[w, k] for k in range(16)]
            if w == 1:
                parts += [XO[k] for k in range(4)]
            return jnp.concatenate(parts, axis=0)

        def up(t):
            cols = pl.ds(t * TILE, TILE)
            acc = jnp.dot(rows(), W[:, cols], preferred_element_type=F32)
            GU[v, cols] = acc
            GUs[v, cols] = acc.astype(BF16)

        def up_half(h):
            up(h)
            up(h + 2)
            for i, t in enumerate((h, h + 2)):
                cols = pl.ds(t * TILE, TILE)
                send(GUs.at[v, cols], GUr.at[v, cols], gid[w][h][i], sibling)

        def hidden(h):
            for i, t in enumerate((h, h + 2)):
                take(GUr.at[v, pl.ds(t * TILE, TILE)], gid[w][h][i], sibling)
            one = pl.ds(h * TILE, TILE)
            two = pl.ds(FF + h * TILE, TILE)

            @pl.loop(0, size // 32)
            def _(i):
                r = pl.ds(pl.multiple_of(lo + i * 32, 32), 32)
                gate = GU[r, one] + GUr[r, one].astype(F32)
                upward = GU[r, two] + GUr[r, two].astype(F32)
                H[r, one] = (jax.nn.silu(gate) * upward).astype(BF16)

        def down(t):
            cols = pl.ds(t * TILE, TILE)
            acc = jnp.dot(H[v, :], Wd[:, cols], preferred_element_type=F32).astype(BF16)
            for k in range(16):
                Pb[w, k, :, cols] = acc[16 * k:16 * k + 16]
            if w == 1:
                for k in range(4):
                    PO[k, :, cols] = acc[256 + 16 * k:272 + 16 * k]

        return (
            [lambda: up_half(0), lambda: up_half(1), lambda: hidden(0), lambda: hidden(1)]
            + [lambda t=t: (down(2 * t), down(2 * t + 1)) for t in range(6)]
        )

    def add_into(dst, srcs):
        n = dst.shape[-1]
        for j in range(n // 128):
            s = pl.ds(j * 128, 128)
            acc = dst[:, s].astype(F32)
            for src in srcs:
                acc = acc + src[:, s].astype(F32)
            dst[:, s] = acc.astype(dst.dtype)

    class Scatter:
        def __init__(self, axis, view, size, cut, dbuf, fbuf):
            self.one = lambda r: view(r, 0, cut)
            self.two = lambda r: view(r, cut, size - cut)
            self.whole = lambda r: view(r, 0, size)
            self.dev = {by: steps[axis](by) for by in (1, -1)}
            self.id = [new_id() for _ in range(6)]
            self.d = (dbuf(0).at[:, pl.ds(0, cut)], dbuf(1).at[:, pl.ds(0, size - cut)])
            self.f = (fbuf(0), fbuf(1))
            self.f1 = [f.at[:, pl.ds(0, cut)] for f in self.f]
            self.f2 = [f.at[:, pl.ds(cut, size - cut)] for f in self.f]

        def start(self):
            send(self.one(2), self.d[0], self.id[0], self.dev[1])
            send(self.two(2), self.d[1], self.id[1], self.dev[-1])

        def plain(self):
            send(self.two(1), self.f2[0], self.id[2], self.dev[1])
            send(self.one(-1), self.f1[1], self.id[3], self.dev[-1])

        def mid(self):
            take(self.d[0], self.id[0], self.dev[1])
            add_into(self.one(1), [self.d[0]])
            send(self.one(1), self.f1[0], self.id[4], self.dev[1])
            take(self.d[1], self.id[1], self.dev[-1])
            add_into(self.two(-1), [self.d[1]])
            send(self.two(-1), self.f2[1], self.id[5], self.dev[-1])

        def fin(self):
            take(self.f2[0], self.id[2], self.dev[1])
            take(self.f1[1], self.id[3], self.dev[-1])
            take(self.f1[0], self.id[4], self.dev[1])
            take(self.f2[1], self.id[5], self.dev[-1])
            add_into(self.whole(0), self.f)

    rid = {k: (new_id(), new_id()) for k in (1, 2, 3)}

    def scatters(w):
        fa, ca, cb = FA[w], CUT_A[w], CUT_B[w]
        fb = HALF - fa
        Pw = Pb.at[w]
        wa, wb = pl.ds(0, fa), pl.ds(0, fb)
        a1, b1 = {}, {}
        for i, k in enumerate(ORDER):
            a1[k] = Scatter(
                "x", lambda r, lo, n, k=k: Pw.at[blk(r, k), :, pl.ds(lo, n)], fa, ca,
                lambda s, i=i: ad.at[w, i, s], lambda s, i=i: af.at[w, i, s, :, wa],
            )
            b1[k] = Scatter(
                "y", lambda r, lo, n, k=k: Pw.at[blk(k, r), :, pl.ds(fa + lo, n)], fb, cb,
                lambda s, i=i: bd.at[w, i, s], lambda s, i=i: bf.at[w, i, s, :, wb],
            )
        a2 = Scatter(
            "y", lambda r, lo, n: Pw.at[blk(0, r), :, pl.ds(lo, n)], fa, ca,
            lambda s: ad2.at[w, s], lambda s: af2.at[w, s, :, wa],
        )
        b2 = Scatter(
            "x", lambda r, lo, n: Pw.at[blk(r, 0), :, pl.ds(fa + lo, n)], fb, cb,
            lambda s: bd2.at[w, s], lambda s: bf2.at[w, s, :, wb],
        )
        if w == 1:
            o1 = Scatter(
                "x", lambda r, lo, n: PO.at[near(x, r), :, pl.ds(lo, n)], HALF, HALF // 2,
                lambda s: od.at[s], lambda s: of.at[s],
            )
            o2 = Scatter(
                "y", lambda r, lo, n: PS.at[near(y, r), :, pl.ds(lo, n)], HALF, HALF // 2,
                lambda s: od2.at[s], lambda s: of2.at[s],
            )
        back = (2, 1, -1, 0)

        def start():
            if w == 1:
                o1.start()
            for k in back:
                a1[k].start()
                b1[k].start()
            if w == 1:
                o1.plain()
            for k in back:
                a1[k].plain()
                b1[k].plain()

        def over_mid():
            o1.mid()

        def mid(k):
            a1[k].mid()
            b1[k].mid()

        def far():
            a1[2].fin()
            a2.start()
            b1[2].fin()
            b2.start()

        def over():
            o1.fin()
            own = PO[x].astype(F32)
            for k in range(4):
                PS[k] = own[4 * k:4 * k + 4]
            o2.start()
            o2.plain()

        def sides():
            for k in (1, -1):
                a1[k].fin()
                b1[k].fin()
            a2.plain()
            b2.plain()

        def cross():
            a2.mid()
            b2.mid()

        def over_cross():
            o2.mid()

        def finish():
            a1[0].fin()
            b1[0].fin()
            a2.fin()
            b2.fin()
            if w == 1:
                o2.fin()

        def home():
            for n in range(4):
                at = lanes(n, 768)
                whole = Pw[here, :, at].astype(F32)
                rzs[w, 0, :, at] = whole[0:8].astype(BF16)
                rzs[w, 1, :, at] = whole[8:16].astype(BF16)
            if w == 0:
                send(rzs.at[0, 1], rzr.at[3], rid[3][0], (c, chip(dz=-1)))
            else:
                send(rzs.at[1, 1], rzr.at[2], rid[2][0], (c, chip(dz=2)))
                send(rzs.at[1, 0], rzr.at[1], rid[1][0], (c, chip(dz=1)))
                for s in range(4):
                    rzos[s] = PS[y, s:s + 1, :]
                for s, k in ((2, 2), (1, 3), (3, 1)):
                    send(rzos.at[s], rzor.at[k], rid[k][1], (c, chip(dz=k)))

        if w == 0:
            return [start] + [lambda k=k: mid(k) for k in back] + [far, sides, cross, finish, home]
        return (
            [start, over_mid] + [lambda k=k: mid(k) for k in back]
            + [over, far, sides, over_cross, cross, finish, home]
        )

    g0, g1 = gathers(0), gathers(1)
    x0, x1 = experts(0), experts(1)
    s0, s1 = scatters(0), scatters(1)

    def run(*todo):
        for f in todo:
            f()

    run(*g0[:4])
    second_wave()
    run(*g0[4:6])
    run(g1[0])
    run(*g0[6:])
    for copy in local[6:]:
        copy.wait()
    run(g1[1], x0[0], g1[2], g1[3], x0[1], g1[4], g1[5], x0[2], x0[3], g1[6])
    run(x0[4], x0[5], g1[7], x0[6], x0[7], g1[8], x0[8], x0[9])
    run(g1[9])
    gathered = len(sent)
    run(s0[0], g1[10])
    run(x1[0], s0[1], s0[2], x1[1], s0[3], s0[4], x1[2], x1[3], s0[5], s0[6])
    run(x1[4], x1[5], s0[7], x1[6], x1[7], x1[8], x1[9])
    run(s1[0])
    flush(gathered)
    run(s0[8], s0[9])
    begun = len(sent)
    run(*s1[1:10])
    flush(begun)
    run(s1[10])
    crossed = len(sent)
    run(*s1[11:])
    flush(crossed)

    rzr[0] = rzs[0, 0]
    rzor[0] = rzos[0]
    for k in (3, 1, 2):
        take(rzr.at[k], rid[k][0], (c, chip(dz=k)))
        take(rzor.at[k], rid[k][1], (c, chip(dz=k)))
    take0 = pick0[:, 0:48].astype(BF16)
    take1 = pick1[:, 0:48].astype(BF16)
    behind = [lax.rem(z - e + 4, 4) for e in range(4)]
    written = []
    for n in range(4):
        at = lanes(n, 768)
        rows = jnp.concatenate(
            [rzr[behind[e], :, at].astype(F32) for e in range(4)]
            + [rzor[behind[e], :, at] for e in range(4)]
            + [jnp.zeros((12, 768), F32)],
            axis=0,
        ).astype(BF16)
        first = jnp.dot(take0, rows, preferred_element_type=F32)
        second = jnp.dot(take1, rows, preferred_element_type=F32)
        layer = hb[:, at].astype(F32) + w0 * first + w1 * second
        for r in range(4):
            ob[r, :, at] = layer[4 * r:4 * r + 4].astype(BF16)
        copy = pltpu.make_async_copy(ob.at[:, :, at], out.at[:, :, at], lsem.at[n])
        copy.start()
        written.append(copy)

    assert counter[0] <= NSEM
    flush(len(sent))
    for copy in written:
        copy.wait()


def shards(
    queries, cache_keys, cache_values, lengths, new_keys, new_values, residual, norm_gain,
    expert_ids, gate_logits, w_gate, w_up, w_down,
):
    hbm = pl.BlockSpec(memory_space=pl.ANY)
    vmem = pl.BlockSpec(memory_space=pltpu.VMEM)
    smem = pl.BlockSpec(memory_space=pltpu.SMEM)
    V = pltpu.VMEM
    rows = 576
    return pl.pallas_call(
        kernel,
        out_shape=jax.ShapeDtypeStruct((4, 4, HALF), BF16),
        in_specs=[smem, hbm, hbm, hbm, hbm, hbm, hbm, vmem, vmem, vmem, hbm, hbm, hbm],
        out_specs=pl.BlockSpec(memory_space=pltpu.HBM),
        scratch_shapes=[
            V((4, 4, HALF), BF16), V((4, 4, HALF), BF16), V((4, 128, 512), BF16), V((4, 128, 512), BF16),
            V((4, 4, 512), BF16), V((4, 4, 512), BF16), V((4, 4, HALF), BF16),
            V((16, HALF), BF16), V((16, HALF), BF16), V((16, 128), F32), V((16, 128), F32),
            V((4, 8, HALF), BF16), V((4, 8, HALF), BF16), V((4, 1, HALF), F32), V((4, 1, HALF), F32),
            V((WAVES, 16, 16, HALF), BF16), V((4, 4, HALF), F32), V((4, 16, HALF), BF16),
            V((HALF, 2 * FF), BF16), V((FF, HALF), BF16),
            V((rows, 2 * FF), F32), V((rows, 2 * FF), BF16), V((rows, 2 * FF), BF16), V((rows, FF), BF16),
            V((WAVES, 16, 16, HALF), BF16), V((4, 16, HALF), BF16), V((4, 4, HALF), F32),
            V((WAVES, 4, 2, 16, 768), BF16), V((WAVES, 4, 2, 16, 1536), BF16),
            V((WAVES, 2, 16, 768), BF16), V((WAVES, 2, 16, 1536), BF16),
            V((WAVES, 4, 2, 16, 896), BF16), V((WAVES, 4, 2, 16, 1792), BF16),
            V((WAVES, 2, 16, 896), BF16), V((WAVES, 2, 16, 1792), BF16),
            V((2, 16, 1536), BF16), V((2, 16, HALF), BF16), V((2, 4, 1536), F32), V((2, 4, HALF), F32),
            V((WAVES, 2, 8, HALF), BF16), V((4, 8, HALF), BF16), V((4, 1, HALF), F32), V((4, 1, HALF), F32),
            pltpu.SemaphoreType.DMA((9,)), pltpu.SemaphoreType.DMA((NSEM,)), pltpu.SemaphoreType.DMA((NSEM,)),
        ],
        compiler_params=pltpu.CompilerParams(collective_id=0, has_side_effects=True),
        name="layer",
    )(
        lengths, queries, cache_keys, cache_values, new_keys, new_values, residual,
        norm_gain.reshape(48, 128), expert_ids.T, gate_logits.T, w_gate, w_up, w_down,
    )


def solution(mesh):
    return jax.shard_map(
        shards,
        mesh=mesh,
        in_specs=(
            P("dev", None, None),
            P("dev", None, None),
            P("dev", None, None),
            P("dev"),
            P("dev", None, None),
            P("dev", None, None),
            P("dev", None, None),
            P(),
            P("dev", None),
            P("dev", None),
            P(None, "dev"),
            P(None, "dev"),
            P("dev", None),
        ),
        out_specs=P("dev", None, "sec"),
        check_vma=False,
    )
```

```python
import jax
import jax.numpy as jnp
from jax import lax
from jax.experimental import pallas as pl
from jax.experimental.pallas import tpu as pltpu
from jax.sharding import PartitionSpec as P

HD = 128
EPS = 1e-05

F32 = jnp.float32
BF16 = jnp.bfloat16
HALF = 3072
FF = 512
NSEM = 288
TILE = 256
WAVES = 2
FA = (1536, 1280)
CUT_A = (768, 640)
CUT_B = (768, 896)
ORDER = (0, 1, -1, 2)
BLOCKS = tuple((i, j) for i in range(4) for j in range(4))


def lanes(j, n=128):
    return slice(j * n, (j + 1) * n)


def kernel(
    lens, q_hbm, k_hbm, v_hbm, nk_hbm, nv_hbm, res_hbm, gain, ids, logits, wg_hbm, wu_hbm, wd_hbm,
    out,
    ob, qb, kb, vb, nkb, nvb, resb, hb, xn, ssb, ssr,
    zs, zr, zos, zor, X, XOs, XO, W, Wd, GU, GUs, GUr, H, Pb, PO, PS,
    ad, af, ad2, af2, bd, bf, bd2, bf2, od, of, od2, of2, rzs, rzr, rzos, rzor,
    lsem, ssem, rsem,
):
    c = lax.axis_index("sec")
    d = lax.axis_index("dev")
    z = d // 16
    x = (d // 4) % 4
    y = d % 4
    here = x * 4 + y

    def near(v, by):
        return lax.rem(v + (by % 4), 4)

    def chip(dz=0, dx=0, dy=0):
        return near(z, dz) * 16 + near(x, dx) * 4 + near(y, dy)

    steps = {"x": lambda by: (c, chip(dx=by)), "y": lambda by: (c, chip(dy=by))}
    zpeers = [(c, chip(dz=k)) for k in (1, 2, 3)]
    sibling = (1 - c, d)
    partners = zpeers + [sibling] + [steps[a](by) for a in ("x", "y") for by in (1, -1)]

    barrier = pltpu.get_barrier_semaphore()
    for p in partners:
        pl.semaphore_signal(barrier, inc=1, device_id=p, device_id_type=pl.DeviceIdType.MESH)

    feats = pl.ds(pl.multiple_of(c * HALF, HALF), HALF)
    kvs = pl.ds(pl.multiple_of(c * 512, 512), 512)
    local = []
    for i, (src, dst) in enumerate((
        (q_hbm.at[:, :, feats], qb),
        (k_hbm.at[:, :, kvs], kb),
        (nk_hbm.at[:, :, kvs], nkb),
        (v_hbm.at[:, :, kvs], vb),
        (nv_hbm.at[:, :, kvs], nvb),
        (res_hbm.at[:, :, feats], resb),
        (wg_hbm.at[feats, :], W.at[:, pl.ds(0, FF)]),
        (wu_hbm.at[feats, :], W.at[:, pl.ds(FF, FF)]),
        (wd_hbm.at[:, feats], Wd),
    )):
        copy = pltpu.make_async_copy(src, dst, lsem.at[i])
        if i < 6:
            copy.start()
        local.append(copy)

    counter = [0]
    sent = []
    flushed = [0]

    def new_id():
        counter[0] += 1
        return counter[0] - 1

    def send(src, dst, sem, dev):
        copy = pltpu.make_async_remote_copy(
            src_ref=src, dst_ref=dst, send_sem=ssem.at[sem], recv_sem=rsem.at[sem],
            device_id=dev, device_id_type=pl.DeviceIdType.MESH,
        )
        copy.start()
        sent.append(copy)

    def flush(upto):
        for copy in sent[flushed[0]:upto]:
            copy.wait_send()
        flushed[0] = max(flushed[0], upto)

    def take(dst, sem, dev):
        pltpu.make_async_remote_copy(
            src_ref=dst, dst_ref=dst, send_sem=ssem.at[sem], recv_sem=rsem.at[sem],
            device_id=dev, device_id_type=pl.DeviceIdType.MESH,
        ).wait_recv()

    square = (16, 16)
    down_row = lax.broadcasted_iota(jnp.int32, square, 0)
    across = lax.broadcasted_iota(jnp.int32, square, 1)

    def column(ref, k):
        rows = jnp.broadcast_to(ref[k:k + 1, :], square)
        return jnp.sum(jnp.where(down_row == across, rows, jnp.zeros_like(rows)), axis=1, keepdims=True)

    id0, id1 = column(ids, 0), column(ids, 1)
    slot = lax.broadcasted_iota(jnp.int32, (16, 128), 1)
    who = jnp.where(slot < 32, slot // 8, slot - 32)
    rank = jnp.where(slot < 32, slot % 8, 8)
    hit0 = id0 == who
    hit1 = id1 == who
    hit = jnp.where(hit0 | hit1, 1.0, 0.0)
    before = jnp.where(across < down_row, 1.0, 0.0)
    ahead = jnp.dot(before.astype(BF16), hit.astype(BF16), preferred_element_type=F32)
    chosen = ahead == rank.astype(F32)
    pick0 = jnp.where(hit0 & chosen, 1.0, 0.0)
    pick1 = jnp.where(hit1 & chosen, 1.0, 0.0)
    packing = jnp.transpose(pick0 + pick1)[0:48].astype(BF16)
    l0, l1 = column(logits, 0), column(logits, 1)
    top = jnp.maximum(l0, l1)
    e0, e1 = jnp.exp(l0 - top), jnp.exp(l1 - top)
    w0 = e0 / (e0 + e1)
    w1 = e1 / (e0 + e1)

    for copy in local[:6]:
        copy.wait()
    for copy in local[6:]:
        copy.start()
    row = lax.broadcasted_iota(jnp.int32, (96, 128), 0)
    col = lax.broadcasted_iota(jnp.int32, (96, 128), 1)
    lenv = jnp.concatenate([jnp.full((24, 128), lens[r], jnp.int32) for r in range(4)], axis=0)
    in_cache = col < lenv
    row16 = lax.broadcasted_iota(jnp.int32, (96, 16), 0)
    col16 = lax.broadcasted_iota(jnp.int32, (96, 16), 1)
    in_window = (row16 // 24 == col16 // 4) & (col16 % 4 <= row16 % 4)
    scale = HD ** (-0.5)
    ss = jnp.zeros((16, 128), F32)
    contract = (((1,), (1,)), ((), ()))
    for g in range(4):
        qs = [
            jnp.concatenate([qb[r, :, lanes(g * 6 + h)].astype(F32) for h in range(6)], axis=0)
            for r in range(4)
        ]
        sc = jnp.concatenate([
            lax.dot_general(qs[r].astype(BF16), kb[r, :, lanes(g)], contract, preferred_element_type=F32)
            for r in range(4)
        ], axis=0) * scale
        nk = jnp.concatenate([nkb[r, :, lanes(g)].astype(F32) for r in range(4)], axis=0).astype(BF16)
        nv = jnp.concatenate([nvb[r, :, lanes(g)].astype(F32) for r in range(4)], axis=0).astype(BF16)
        qa = jnp.concatenate(qs, axis=0).astype(BF16)
        sn = lax.dot_general(qa, nk, contract, preferred_element_type=F32) * scale
        sc = jnp.where(in_cache, sc, -1e30)
        sn = jnp.where(in_window, sn, -1e30)
        peak = jnp.maximum(jnp.max(sc, axis=1, keepdims=True), jnp.max(sn, axis=1, keepdims=True))
        ec = jnp.exp(sc - peak)
        en = jnp.exp(sn - peak)
        total = jnp.sum(ec, axis=1, keepdims=True) + jnp.sum(en, axis=1, keepdims=True)
        inv = 1.0 / total
        pc = ec * inv
        pn = (en * inv).astype(BF16)
        att = jnp.concatenate([
            jnp.dot(pc[24 * r:24 * r + 24].astype(BF16), vb[r, :, lanes(g)], preferred_element_type=F32)
            for r in range(4)
        ], axis=0) + jnp.dot(pn, nv, preferred_element_type=F32)
        for h in range(6):
            j = g * 6 + h
            part = jnp.concatenate([att[r * 24 + h * 4:r * 24 + h * 4 + 4] for r in range(4)], axis=0)
            res = jnp.concatenate([resb[r, :, lanes(j)].astype(F32) for r in range(4)], axis=0)
            hst = (res + part).astype(BF16)
            hb[:, lanes(j)] = hst
            hf = hst.astype(F32)
            ss = ss + hf * hf
    ssb[...] = jnp.broadcast_to(jnp.sum(ss, axis=1, keepdims=True), (16, 128))
    pl.semaphore_wait(barrier, len(partners))
    sid = new_id()
    send(ssb, ssr, sid, sibling)

    take(ssr, sid, sibling)
    inv = lax.rsqrt((ssb[...] + ssr[...]) / (2 * HALF) + EPS)
    gains = gain[pl.ds(pl.multiple_of(c * 24, 8), 24), :]
    for j in range(24):
        xn[:, lanes(j)] = (hb[:, lanes(j)].astype(F32) * inv * gains[j:j + 1]).astype(BF16)
    for n in range(4):
        at = lanes(n, 768)
        packed = jnp.dot(packing, xn[:, at], preferred_element_type=F32)
        for e in range(4):
            zs[e, :, at] = packed[8 * e:8 * e + 8].astype(BF16)
            zos[e, :, at] = packed[32 + e:33 + e]

    zid = {k: (new_id(), new_id()) for k in (1, 3, 2)}
    for k in (1, 3, 2):
        send(zs.at[near(z, k)], zr.at[k], zid[k][0], (c, chip(dz=k)))
    for k in (1, 3, 2):
        send(zos.at[near(z, k)], zor.at[k], zid[k][1], (c, chip(dz=k)))

    def form(w, first, second):
        for n in range(4):
            at = lanes(n, 768)
            X[w, here, :, at] = jnp.concatenate([first(at).astype(F32), second(at).astype(F32)], axis=0).astype(BF16)

    take(zr.at[1], zid[1][0], (c, chip(dz=1)))
    form(0, lambda at: zs[z, :, at], lambda at: zr[1, :, at])

    def second_wave():
        for k in (3, 2):
            take(zr.at[k], zid[k][0], (c, chip(dz=k)))
        form(1, lambda at: zr[3, :, at], lambda at: zr[2, :, at])
        for k in (1, 3, 2):
            take(zor.at[k], zid[k][1], (c, chip(dz=k)))
        XOs[y, 0:1, :] = zos[z]
        for k in (1, 2, 3):
            XOs[y, k:k + 1, :] = zor[k]

    def blk(dx, dy):
        return near(x, dx) * 4 + near(y, dy)

    class Gather:
        def __init__(self, axis, view, size, cut):
            self.one = lambda r: view(r, 0, cut)
            self.two = lambda r: view(r, cut, size - cut)
            self.dev = {by: steps[axis](by) for by in (1, -1)}
            self.id = [new_id() for _ in range(6)]

        def start(self):
            one, two = self.one(0), self.two(0)
            send(one, one, self.id[0], self.dev[1])
            send(two, two, self.id[1], self.dev[-1])
            send(two, two, self.id[2], self.dev[1])
            send(one, one, self.id[3], self.dev[-1])

        def pass_on(self):
            v = self.one(-1)
            take(v, self.id[0], self.dev[1])
            send(v, v, self.id[4], self.dev[1])
            v = self.two(1)
            take(v, self.id[1], self.dev[-1])
            send(v, v, self.id[5], self.dev[-1])

        def rest(self):
            take(self.two(-1), self.id[2], self.dev[1])
            take(self.one(1), self.id[3], self.dev[-1])

        def far(self):
            take(self.one(2), self.id[4], self.dev[1])
            take(self.two(2), self.id[5], self.dev[-1])

    def gathers(w):
        fa, ca, cb = FA[w], CUT_A[w], CUT_B[w]
        fb = HALF - fa
        Xw = X.at[w]
        a1 = Gather("y", lambda r, lo, n: Xw.at[blk(0, r), :, pl.ds(lo, n)], fa, ca)
        b1 = Gather("x", lambda r, lo, n: Xw.at[blk(r, 0), :, pl.ds(fa + lo, n)], fb, cb)
        a2 = {
            k: Gather("x", lambda r, lo, n, k=k: Xw.at[blk(r, k), :, pl.ds(lo, n)], fa, ca) for k in ORDER
        }
        b2 = {
            k: Gather("y", lambda r, lo, n, k=k: Xw.at[blk(k, r), :, pl.ds(fa + lo, n)], fb, cb) for k in ORDER
        }
        if w == 1:
            o1 = Gather("y", lambda r, lo, n: XOs.at[near(y, r), :, pl.ds(lo, n)], HALF, HALF // 2)
            o2 = Gather("x", lambda r, lo, n: XO.at[near(x, r), :, pl.ds(lo, n)], HALF, HALF // 2)

        def start():
            a1.start()
            b1.start()
            if w == 1:
                o1.start()
            a2[0].start()
            b2[0].start()

        def line():
            a1.pass_on()
            b1.pass_on()
            a1.rest()
            a2[1].start()
            b1.rest()
            b2[1].start()
            a2[-1].start()
            b2[-1].start()

        def line_over():
            o1.pass_on()
            o1.rest()

        def own():
            a2[0].pass_on()
            b2[0].pass_on()

        def far_line():
            a1.far()
            a2[2].start()
            b1.far()
            b2[2].start()

        def over():
            o1.far()
            XO[x] = jnp.concatenate([XOs[k] for k in range(4)], axis=0).astype(BF16)
            o2.start()

        def sides(k):
            a2[k].pass_on()
            b2[k].pass_on()

        def over_pass():
            o2.pass_on()

        def finish():
            for k in ORDER:
                a2[k].rest()
                b2[k].rest()
                a2[k].far()
                b2[k].far()
            if w == 1:
                o2.rest()
                o2.far()

        steps_of = [start, line, own, far_line, lambda: sides(1), lambda: sides(-1), lambda: sides(2), finish]
        if w == 1:
            steps_of = [
                start, line, line_over, own, far_line, over, lambda: sides(1), lambda: sides(-1), lambda: sides(2),
                over_pass, finish,
            ]
        return steps_of

    place = ((0, 256), (256, 320))
    gid = [[[new_id(), new_id()] for _ in range(2)] for _ in range(WAVES)]

    def experts(w):
        lo, size = place[w]
        v = pl.ds(lo, size)

        def rows():
            parts = [X[w, k] for k in range(16)]
            if w == 1:
                parts += [XO[k] for k in range(4)]
            return jnp.concatenate(parts, axis=0)

        def up(t):
            cols = pl.ds(t * TILE, TILE)
            acc = jnp.dot(rows(), W[:, cols], preferred_element_type=F32)
            GU[v, cols] = acc
            GUs[v, cols] = acc.astype(BF16)

        def up_half(h):
            up(h)
            up(h + 2)
            for i, t in enumerate((h, h + 2)):
                cols = pl.ds(t * TILE, TILE)
                send(GUs.at[v, cols], GUr.at[v, cols], gid[w][h][i], sibling)

        def hidden(h):
            for i, t in enumerate((h, h + 2)):
                take(GUr.at[v, pl.ds(t * TILE, TILE)], gid[w][h][i], sibling)
            one = pl.ds(h * TILE, TILE)
            two = pl.ds(FF + h * TILE, TILE)

            @pl.loop(0, size // 32)
            def _(i):
                r = pl.ds(pl.multiple_of(lo + i * 32, 32), 32)
                gate = GU[r, one] + GUr[r, one].astype(F32)
                upward = GU[r, two] + GUr[r, two].astype(F32)
                H[r, one] = (jax.nn.silu(gate) * upward).astype(BF16)

        def down(t):
            cols = pl.ds(t * TILE, TILE)
            acc = jnp.dot(H[v, :], Wd[:, cols], preferred_element_type=F32).astype(BF16)
            for k in range(16):
                Pb[w, k, :, cols] = acc[16 * k:16 * k + 16]
            if w == 1:
                for k in range(4):
                    PO[k, :, cols] = acc[256 + 16 * k:272 + 16 * k]

        return (
            [lambda: up_half(0), lambda: up_half(1), lambda: hidden(0), lambda: hidden(1)]
            + [lambda t=t: (down(2 * t), down(2 * t + 1)) for t in range(6)]
        )

    def add_into(dst, srcs):
        n = dst.shape[-1]
        for j in range(n // 128):
            s = pl.ds(j * 128, 128)
            acc = dst[:, s].astype(F32)
            for src in srcs:
                acc = acc + src[:, s].astype(F32)
            dst[:, s] = acc.astype(dst.dtype)

    class Scatter:
        def __init__(self, axis, view, size, cut, dbuf, fbuf):
            self.one = lambda r: view(r, 0, cut)
            self.two = lambda r: view(r, cut, size - cut)
            self.whole = lambda r: view(r, 0, size)
            self.dev = {by: steps[axis](by) for by in (1, -1)}
            self.id = [new_id() for _ in range(6)]
            self.d = (dbuf(0).at[:, pl.ds(0, cut)], dbuf(1).at[:, pl.ds(0, size - cut)])
            self.f = (fbuf(0), fbuf(1))
            self.f1 = [f.at[:, pl.ds(0, cut)] for f in self.f]
            self.f2 = [f.at[:, pl.ds(cut, size - cut)] for f in self.f]

        def start(self):
            send(self.one(2), self.d[0], self.id[0], self.dev[1])
            send(self.two(2), self.d[1], self.id[1], self.dev[-1])

        def plain(self):
            send(self.two(1), self.f2[0], self.id[2], self.dev[1])
            send(self.one(-1), self.f1[1], self.id[3], self.dev[-1])

        def mid(self):
            take(self.d[0], self.id[0], self.dev[1])
            add_into(self.one(1), [self.d[0]])
            send(self.one(1), self.f1[0], self.id[4], self.dev[1])
            take(self.d[1], self.id[1], self.dev[-1])
            add_into(self.two(-1), [self.d[1]])
            send(self.two(-1), self.f2[1], self.id[5], self.dev[-1])

        def fin(self):
            take(self.f2[0], self.id[2], self.dev[1])
            take(self.f1[1], self.id[3], self.dev[-1])
            take(self.f1[0], self.id[4], self.dev[1])
            take(self.f2[1], self.id[5], self.dev[-1])
            add_into(self.whole(0), self.f)

    rid = {k: (new_id(), new_id()) for k in (1, 2, 3)}

    def scatters(w):
        fa, ca, cb = FA[w], CUT_A[w], CUT_B[w]
        fb = HALF - fa
        Pw = Pb.at[w]
        wa, wb = pl.ds(0, fa), pl.ds(0, fb)
        a1, b1 = {}, {}
        for i, k in enumerate(ORDER):
            a1[k] = Scatter(
                "x", lambda r, lo, n, k=k: Pw.at[blk(r, k), :, pl.ds(lo, n)], fa, ca,
                lambda s, i=i: ad.at[w, i, s], lambda s, i=i: af.at[w, i, s, :, wa],
            )
            b1[k] = Scatter(
                "y", lambda r, lo, n, k=k: Pw.at[blk(k, r), :, pl.ds(fa + lo, n)], fb, cb,
                lambda s, i=i: bd.at[w, i, s], lambda s, i=i: bf.at[w, i, s, :, wb],
            )
        a2 = Scatter(
            "y", lambda r, lo, n: Pw.at[blk(0, r), :, pl.ds(lo, n)], fa, ca,
            lambda s: ad2.at[w, s], lambda s: af2.at[w, s, :, wa],
        )
        b2 = Scatter(
            "x", lambda r, lo, n: Pw.at[blk(r, 0), :, pl.ds(fa + lo, n)], fb, cb,
            lambda s: bd2.at[w, s], lambda s: bf2.at[w, s, :, wb],
        )
        if w == 1:
            o1 = Scatter(
                "x", lambda r, lo, n: PO.at[near(x, r), :, pl.ds(lo, n)], HALF, HALF // 2,
                lambda s: od.at[s], lambda s: of.at[s],
            )
            o2 = Scatter(
                "y", lambda r, lo, n: PS.at[near(y, r), :, pl.ds(lo, n)], HALF, HALF // 2,
                lambda s: od2.at[s], lambda s: of2.at[s],
            )
        back = (2, 1, -1, 0)

        def start():
            if w == 1:
                o1.start()
            for k in back:
                a1[k].start()
                b1[k].start()
            if w == 1:
                o1.plain()
            for k in back:
                a1[k].plain()
                b1[k].plain()

        def over_mid():
            o1.mid()

        def mid(k):
            a1[k].mid()
            b1[k].mid()

        def far():
            a1[2].fin()
            a2.start()
            b1[2].fin()
            b2.start()

        def over():
            o1.fin()
            own = PO[x].astype(F32)
            for k in range(4):
                PS[k] = own[4 * k:4 * k + 4]
            o2.start()
            o2.plain()

        def sides():
            for k in (1, -1):
                a1[k].fin()
                b1[k].fin()
            a2.plain()
            b2.plain()

        def cross():
            a2.mid()
            b2.mid()

        def over_cross():
            o2.mid()

        def finish():
            a1[0].fin()
            b1[0].fin()
            a2.fin()
            b2.fin()
            if w == 1:
                o2.fin()

        def home():
            for n in range(4):
                at = lanes(n, 768)
                whole = Pw[here, :, at].astype(F32)
                rzs[w, 0, :, at] = whole[0:8].astype(BF16)
                rzs[w, 1, :, at] = whole[8:16].astype(BF16)
            if w == 0:
                send(rzs.at[0, 1], rzr.at[3], rid[3][0], (c, chip(dz=-1)))
            else:
                send(rzs.at[1, 1], rzr.at[2], rid[2][0], (c, chip(dz=2)))
                send(rzs.at[1, 0], rzr.at[1], rid[1][0], (c, chip(dz=1)))
                for s in range(4):
                    rzos[s] = PS[y, s:s + 1, :]
                for s, k in ((2, 2), (1, 3), (3, 1)):
                    send(rzos.at[s], rzor.at[k], rid[k][1], (c, chip(dz=k)))

        if w == 0:
            return [start] + [lambda k=k: mid(k) for k in back] + [far, sides, cross, finish, home]
        return (
            [start, over_mid] + [lambda k=k: mid(k) for k in back]
            + [over, far, sides, over_cross, cross, finish, home]
        )

    g0, g1 = gathers(0), gathers(1)
    x0, x1 = experts(0), experts(1)
    s0, s1 = scatters(0), scatters(1)

    def run(*todo):
        for f in todo:
            f()

    run(*g0[:4])
    second_wave()
    run(g1[0])
    run(*g0[4:])
    for copy in local[6:]:
        copy.wait()
    run(g1[1], x0[0], g1[2], g1[3], x0[1], g1[4], g1[5], x0[2], x0[3], g1[6])
    run(x0[4], x0[5], g1[7], x0[6], x0[7], g1[8], x0[8], x0[9])
    run(g1[9])
    gathered = len(sent)
    run(s0[0], g1[10])
    run(x1[0], s0[1], s0[2], x1[1], s0[3], s0[4], x1[2], x1[3], s0[5], s0[6])
    run(x1[4], x1[5], s0[7], x1[6], x1[7], x1[8], x1[9])
    run(s1[0])
    flush(gathered)
    run(s0[8], s0[9])
    begun = len(sent)
    run(*s1[1:10])
    flush(begun)
    run(s1[10])
    crossed = len(sent)
    run(*s1[11:])
    flush(crossed)

    rzr[0] = rzs[0, 0]
    rzor[0] = rzos[0]
    for k in (3, 1, 2):
        take(rzr.at[k], rid[k][0], (c, chip(dz=k)))
        take(rzor.at[k], rid[k][1], (c, chip(dz=k)))
    take0 = pick0[:, 0:48].astype(BF16)
    take1 = pick1[:, 0:48].astype(BF16)
    behind = [lax.rem(z - e + 4, 4) for e in range(4)]
    written = []
    for n in range(4):
        at = lanes(n, 768)
        rows = jnp.concatenate(
            [rzr[behind[e], :, at].astype(F32) for e in range(4)]
            + [rzor[behind[e], :, at] for e in range(4)]
            + [jnp.zeros((12, 768), F32)],
            axis=0,
        ).astype(BF16)
        first = jnp.dot(take0, rows, preferred_element_type=F32)
        second = jnp.dot(take1, rows, preferred_element_type=F32)
        layer = hb[:, at].astype(F32) + w0 * first + w1 * second
        for r in range(4):
            ob[r, :, at] = layer[4 * r:4 * r + 4].astype(BF16)
        copy = pltpu.make_async_copy(ob.at[:, :, at], out.at[:, :, at], lsem.at[n])
        copy.start()
        written.append(copy)

    assert counter[0] <= NSEM
    flush(len(sent))
    for copy in written:
        copy.wait()


def shards(
    queries, cache_keys, cache_values, lengths, new_keys, new_values, residual, norm_gain,
    expert_ids, gate_logits, w_gate, w_up, w_down,
):
    hbm = pl.BlockSpec(memory_space=pl.ANY)
    vmem = pl.BlockSpec(memory_space=pltpu.VMEM)
    smem = pl.BlockSpec(memory_space=pltpu.SMEM)
    V = pltpu.VMEM
    rows = 576
    return pl.pallas_call(
        kernel,
        out_shape=jax.ShapeDtypeStruct((4, 4, HALF), BF16),
        in_specs=[smem, hbm, hbm, hbm, hbm, hbm, hbm, vmem, vmem, vmem, hbm, hbm, hbm],
        out_specs=pl.BlockSpec(memory_space=pltpu.HBM),
        scratch_shapes=[
            V((4, 4, HALF), BF16), V((4, 4, HALF), BF16), V((4, 128, 512), BF16), V((4, 128, 512), BF16),
            V((4, 4, 512), BF16), V((4, 4, 512), BF16), V((4, 4, HALF), BF16),
            V((16, HALF), BF16), V((16, HALF), BF16), V((16, 128), F32), V((16, 128), F32),
            V((4, 8, HALF), BF16), V((4, 8, HALF), BF16), V((4, 1, HALF), F32), V((4, 1, HALF), F32),
            V((WAVES, 16, 16, HALF), BF16), V((4, 4, HALF), F32), V((4, 16, HALF), BF16),
            V((HALF, 2 * FF), BF16), V((FF, HALF), BF16),
            V((rows, 2 * FF), F32), V((rows, 2 * FF), BF16), V((rows, 2 * FF), BF16), V((rows, FF), BF16),
            V((WAVES, 16, 16, HALF), BF16), V((4, 16, HALF), BF16), V((4, 4, HALF), F32),
            V((WAVES, 4, 2, 16, 768), BF16), V((WAVES, 4, 2, 16, 1536), BF16),
            V((WAVES, 2, 16, 768), BF16), V((WAVES, 2, 16, 1536), BF16),
            V((WAVES, 4, 2, 16, 896), BF16), V((WAVES, 4, 2, 16, 1792), BF16),
            V((WAVES, 2, 16, 896), BF16), V((WAVES, 2, 16, 1792), BF16),
            V((2, 16, 1536), BF16), V((2, 16, HALF), BF16), V((2, 4, 1536), F32), V((2, 4, HALF), F32),
            V((WAVES, 2, 8, HALF), BF16), V((4, 8, HALF), BF16), V((4, 1, HALF), F32), V((4, 1, HALF), F32),
            pltpu.SemaphoreType.DMA((9,)), pltpu.SemaphoreType.DMA((NSEM,)), pltpu.SemaphoreType.DMA((NSEM,)),
        ],
        compiler_params=pltpu.CompilerParams(collective_id=0, has_side_effects=True),
        name="layer",
    )(
        lengths, queries, cache_keys, cache_values, new_keys, new_values, residual,
        norm_gain.reshape(48, 128), expert_ids.T, gate_logits.T, w_gate, w_up, w_down,
    )


def solution(mesh):
    return jax.shard_map(
        shards,
        mesh=mesh,
        in_specs=(
            P("dev", None, None),
            P("dev", None, None),
            P("dev", None, None),
            P("dev"),
            P("dev", None, None),
            P("dev", None, None),
            P("dev", None, None),
            P(),
            P("dev", None),
            P("dev", None),
            P(None, "dev"),
            P(None, "dev"),
            P("dev", None),
        ),
        out_specs=P("dev", None, "sec"),
        check_vma=False,
    )
```
